128 devices in a mesh: dp: 2 (over x_hi), pipe: 2 (over core), expert: 32 (over z, y, x_lo).
Axes of the slice: x: 4 (x_hi: 2, x_lo: 2; x = x_hi * 2 + x_lo), y: 4, z: 4, core: 2. Of those that a mesh axis runs over, the one named last changes fastest.
Arguments:
- inputs: bfloat16 [4, 2048, 1024], P(None, ('dp', 'expert')), may hold values from -6 to 6
- cotangent: bfloat16 [4, 2048, 1024], P(None, ('dp', 'expert')), may hold values from -0.29882812 to 0.29882812
- norm_gain: float32 [2, 1024], P('pipe'), may hold values from 0.5 to 1.5
- w_router: bfloat16 [2, 1024, 32], P('pipe'), may hold values from -0.1875 to 0.1875
- w_gate: bfloat16 [2, 32, 1024, 512], P('pipe', 'expert'), may hold values from -0.1875 to 0.1875
- w_up: bfloat16 [2, 32, 1024, 512], P('pipe', 'expert'), may hold values from -0.1875 to 0.1875
- w_down: bfloat16 [2, 32, 512, 1024], P('pipe', 'expert'), may hold values from -0.25 to 0.25
- routes: int32 [2, 4, 2048, 8], P('pipe', None, ('dp', 'expert')), may hold values from 0 to 31, all different within a row; in each aligned block of 32 rows (0 to 31, 32 to 63, ..., all dimensions but the last counted through in order) at most 10 rows name the same one
Outputs:
- grad_gate: bfloat16 [2, 32, 1024, 512], P('pipe', 'expert', 'dp')
- grad_up: bfloat16 [2, 32, 1024, 512], P('pipe', 'expert', 'dp')
- grad_down: bfloat16 [2, 32, 512, 1024], P('pipe', 'expert', None, 'dp')
- grad_router: float32 [2, 1024, 32], P('pipe')
- grad_gain: float32 [2, 1024], P('pipe')
The draws below stay inside these ranges and needn't reach their ends.
Inputs may be any that keep to these rules, and one draw needn't show every extreme that they name: `routes`: the experts of a token differ. Among the 32 tokens of one device in one layer and micro-batch, no expert is picked by more than 10 tokens, and some expert is picked by exactly 10 in some of them.
All inputs are finite; a program needn't handle non-finite values.
Results may differ from the reference program's by a relative error of at most 0.012.
Values may be sent and summed in bfloat16 or wider, within the bound.
No kernel may reach another device: no remote copies, remote signals or barrier semaphores. Data moves between devices by JAX's collectives and lax.ppermute only.
A program may use at most 128 MiB of HBM per device.

```python
import math
import jax
import jax.numpy as jnp
import numpy as np
from jax import lax

D = 1024
TOP = 8
FF_DEV = 512
TOK_MB = 32
MICRO = 4
LAYERS = 2
EXPERTS = 32
TOKENS = 2048
CAP = 10
N_DP = 2
N_EXPERT = 32


def block_levels(key, extent, split, low, largest):
    def one(position, shards_of):
        draws = jax.random.uniform(jax.random.fold_in(jax.random.fold_in(key, 6), position), (shards_of,), jnp.float32, low / len(split), largest / len(split))
        return jnp.repeat(jnp.exp(draws), extent[position] // shards_of).reshape((-1,) + (1,) * (len(extent) - position - 1))

    level = one(*split[0])
    for cut in split[1:]:
        level = level * one(*cut)
    return level


def shared_out(stream_key, own, number, rows, number_of, top, reach, skew):
    sequence = jax.random.permutation(stream_key, number_of)
    heavy_load, usual = portions_of(number_of, rows * top, reach, skew, True), portions_of(number_of, rows * top, reach, skew, False)
    places = jnp.arange(number_of)

    def named(lengths, rotation):
        used = int((lengths > 0).sum())
        fixed = max(1, used // 4)
        passed = fixed + (places - fixed + rotation * (used - fixed)) % max(1, number_of - fixed)
        return jnp.zeros((number_of,), jnp.int32).at[sequence[jnp.where(places < fixed, places, passed)]].set(jnp.asarray(lengths, jnp.int32))

    lengths = jnp.where(number % 4 == 0, named(heavy_load, number // 4), named(usual, number - number // 4 - 1))
    mixed = jax.random.permutation(jax.random.fold_in(own, 3), number_of)
    giver, sink = mixed[0:number_of // 2 * 2:2], mixed[1:number_of // 2 * 2:2]
    slack = jnp.minimum(lengths[giver] - 1, reach - lengths[sink]) // 2
    slack = jnp.where((giver == sequence[0]) | (sink == sequence[0]) | (lengths[sink] == 0), 0, jnp.maximum(slack, 0))
    passed = jax.random.randint(jax.random.fold_in(own, 4), (number_of // 2,), 0, 1 << 20) % (slack + 1)
    lengths = lengths.at[giver].add(-passed).at[sink].add(passed)
    labels = jnp.searchsorted(jnp.cumsum(lengths), jnp.arange(rows * top), side="right").astype(jnp.int32)
    table = labels.reshape(top, rows).T
    table = table[jax.random.permutation(jax.random.fold_in(own, 1), rows)]
    rotation = jax.random.randint(jax.random.fold_in(own, 2), (rows, 1), 0, top)
    return jnp.take_along_axis(table, (jnp.arange(top)[None, :] + rotation) % top, axis=1)


def portions_of(amount, total, bound, skew, full):
    portions = [(1 << 20) // math.isqrt(grade ** skew) + 1 for grade in range(1, amount + 1)]
    largest = bound if full else min(bound, max(-(-total // amount), total * portions[0] // sum(portions)))
    least = 1 if total - largest >= amount - 1 else 0
    counts, surplus = [largest] + [least] * (amount - 1), total - largest - least * (amount - 1)
    while surplus > 0:
        candidates = [i for i in range(1, amount) if counts[i] < largest] or [i for i in range(1, amount) if counts[i] < bound]
        pool, budget = sum([portions[i] for i in candidates]), surplus
        for i in candidates:
            more = min(bound - counts[i], max(1, budget * portions[i] // pool), surplus)
            counts[i] = counts[i] + more
            surplus = surplus - more
    return np.array(counts)


def centred(stream_key, shape, deviation, reach, cuts=(), kind=jnp.bfloat16):
    factor_of = block_levels(stream_key, shape, cuts, -0.22, 0.18) if cuts else 1.0
    drawn = jax.random.normal(stream_key, shape, jnp.float32) * deviation * factor_of
    return jnp.minimum(jnp.maximum(drawn, -reach), reach).astype(kind)


def setup_inputs(seed: int = 0) -> dict:
    key_list = jax.random.split(jax.random.key(seed), 9)
    inputs = centred(key_list[0], (MICRO, TOKENS, D), 1.0, 6.0, ((1, 64),))
    cotangent = centred(key_list[1], (MICRO, TOKENS, D), 0.05, 0.29882812, ((1, 64),))
    norm_gain = jnp.clip(1.0 + 0.1 * jax.random.normal(key_list[2], (LAYERS, D), jnp.float32), 0.5, 1.5)
    w_router = centred(key_list[3], (LAYERS, D, EXPERTS), D ** -0.5, 0.1875, ((0, 2),))
    w_gate = centred(key_list[4], (LAYERS, EXPERTS, D, FF_DEV), D ** -0.5, 0.1875, ((0, 2), (1, 32)))
    w_up = centred(key_list[5], (LAYERS, EXPERTS, D, FF_DEV), D ** -0.5, 0.1875, ((0, 2), (1, 32)))
    w_down = centred(key_list[6], (LAYERS, EXPERTS, FF_DEV, D), FF_DEV ** -0.5, 0.25, ((0, 2), (1, 32)))
    routes_keys = jax.random.split(jax.random.fold_in(key_list[7], 1), LAYERS * MICRO * TOKENS // TOK_MB)
    routes_turns = jax.random.permutation(jax.random.fold_in(key_list[7], 3), LAYERS * MICRO * TOKENS // TOK_MB)
    routes = jax.vmap(lambda own, number: shared_out(jax.random.fold_in(key_list[7], 2), own, number, TOK_MB, EXPERTS, TOP, CAP, 2))(routes_keys, routes_turns).reshape((LAYERS, MICRO, TOKENS, TOP))
    return {"inputs": inputs, "cotangent": cotangent, "norm_gain": norm_gain, "w_router": w_router, "w_gate": w_gate, "w_up": w_up, "w_down": w_down, "routes": routes}


EPS = 1e-05

def block_tables(picks):
    onehot = (picks[..., None] == jnp.arange(EXPERTS, dtype=jnp.int32)).astype(jnp.int32)
    flat = onehot.reshape(picks.shape[0], -1, EXPERTS)
    before = jnp.cumsum(flat, axis=1) - flat
    slot = lax.optimization_barrier(jnp.sum(before * flat, axis=-1)).reshape(picks.shape)
    return (onehot, slot)

def expert_pass(items):
    rows_in, gate_mat, up_mat, down_mat = items
    gate_act = jnp.dot(rows_in, gate_mat, preferred_element_type=jnp.float32)
    up_act = jnp.dot(rows_in, up_mat, preferred_element_type=jnp.float32)
    hidden = (jax.nn.silu(gate_act) * up_act).astype(jnp.bfloat16)
    output = jnp.dot(hidden, down_mat, preferred_element_type=jnp.float32).astype(jnp.bfloat16)
    return (gate_act, up_act, hidden, output)

def layer_pieces(tokens, picks, gain, router, gate_w, up_w, down_w):
    blocks = tokens.shape[0]
    per_expert = blocks * CAP
    values = tokens.astype(jnp.float32)
    scale = lax.rsqrt(lax.optimization_barrier(jnp.mean(values * values, axis=-1, keepdims=True)) + EPS)
    normed = (values * scale * gain).astype(jnp.bfloat16)
    onehot, slot = block_tables(picks)
    block_ids = jnp.arange(blocks, dtype=jnp.int32)[:, None, None]
    index = (picks * per_expert + block_ids * CAP + slot).astype(jnp.int32).reshape(-1)
    spread = jnp.broadcast_to(normed[:, :, None, :], picks.shape + (D,)).reshape(-1, D)
    buffer = jnp.zeros((EXPERTS * per_expert, D), jnp.bfloat16).at[index].set(spread)
    buffer = buffer.reshape(EXPERTS, per_expert, D)
    gate_act, up_act, hidden, output = lax.map(expert_pass, (buffer, gate_w, up_w, down_w))
    chosen = output.reshape(-1, D)[index].reshape(picks.shape + (D,)).astype(jnp.float32)
    logits = jnp.dot(normed.reshape(-1, D), router, preferred_element_type=jnp.float32)
    logits = logits.reshape(blocks, TOK_MB, EXPERTS)
    picked = lax.optimization_barrier(jnp.sum(logits[:, :, None, :] * onehot.astype(jnp.float32), axis=-1))
    expo = jnp.exp(picked)
    weights = expo / lax.optimization_barrier(jnp.sum(expo, axis=-1, keepdims=True))
    return (values, scale, normed, onehot, index, buffer, gate_act, up_act, hidden, chosen, weights)

def layer_forward(tokens, picks, gain, router, gate_w, up_w, down_w):
    pieces = layer_pieces(tokens, picks, gain, router, gate_w, up_w, down_w)
    values, chosen, weights = (pieces[0], pieces[9], pieces[10])
    mixed = values + lax.optimization_barrier(jnp.sum(weights[..., None] * chosen, axis=-2))
    return mixed.astype(jnp.bfloat16)

def group_partial(left, right):
    left_groups = jnp.swapaxes(left.reshape(MICRO, N_DP, -1, left.shape[-1]), 0, 1).reshape(N_DP, -1, left.shape[-1])
    right_groups = jnp.swapaxes(right.reshape(MICRO, N_DP, -1, right.shape[-1]), 0, 1).reshape(N_DP, -1, right.shape[-1])
    total = jnp.zeros((left.shape[-1], right.shape[-1]), jnp.float32)
    for group in range(N_DP):
        term = jnp.dot(left_groups[group].T, right_groups[group], preferred_element_type=jnp.float32)
        total = total + lax.optimization_barrier(term.astype(jnp.bfloat16)).astype(jnp.float32)
    return total.astype(jnp.bfloat16)

def expert_back(items):
    rows_in, gate_act, up_act, hidden, grad_rows, gate_mat, up_mat, down_mat = items
    grad_hidden = jnp.dot(grad_rows, down_mat.T, preferred_element_type=jnp.float32)
    sig = jax.nn.sigmoid(gate_act)
    gate_back = (grad_hidden * up_act * sig * (1.0 + gate_act * (1.0 - sig))).astype(jnp.bfloat16)
    up_back = (grad_hidden * gate_act * sig).astype(jnp.bfloat16)
    back_rows = (jnp.dot(gate_back, gate_mat.T, preferred_element_type=jnp.float32) + jnp.dot(up_back, up_mat.T, preferred_element_type=jnp.float32)).astype(jnp.bfloat16)
    return (back_rows, group_partial(rows_in, gate_back), group_partial(rows_in, up_back), group_partial(hidden, grad_rows))

def layer_backward(grad_out, tokens, picks, gain, router, gate_w, up_w, down_w):
    values, scale, normed, onehot, index, buffer, gate_act, up_act, hidden, chosen, weights = layer_pieces(tokens, picks, gain, router, gate_w, up_w, down_w)
    blocks = tokens.shape[0]
    grad_f = grad_out.astype(jnp.float32)
    weight_grad = lax.optimization_barrier(jnp.sum(grad_f[:, :, None, :] * chosen, axis=-1))
    scaled = (weights[..., None] * grad_f[:, :, None, :]).astype(jnp.bfloat16)
    grad_buffer = jnp.zeros((EXPERTS * blocks * CAP, D), jnp.bfloat16).at[index].set(scaled.reshape(-1, D))
    grad_buffer = grad_buffer.reshape(EXPERTS, blocks * CAP, D)
    back, gate_grad, up_grad, down_grad = lax.map(expert_back, (buffer, gate_act, up_act, hidden, grad_buffer, gate_w, up_w, down_w))
    returned = back.reshape(-1, D)[index].reshape(picks.shape + (D,)).astype(jnp.float32)
    logit_grad = weights * (weight_grad - lax.optimization_barrier(jnp.sum(weights * weight_grad, axis=-1, keepdims=True)))
    logits_grad = lax.optimization_barrier(jnp.sum(logit_grad[..., None] * onehot.astype(jnp.float32), axis=-2))
    logits_grad = logits_grad.astype(jnp.bfloat16).reshape(-1, EXPERTS)
    router_grad = jnp.dot(normed.reshape(-1, D).T, logits_grad, preferred_element_type=jnp.float32)
    normed_grad = jnp.dot(logits_grad, router.T, preferred_element_type=jnp.float32).reshape(blocks, TOK_MB, D)
    normed_grad = normed_grad + lax.optimization_barrier(jnp.sum(returned, axis=-2))
    gain_grad = lax.optimization_barrier(jnp.sum((normed_grad * values * scale).reshape(-1, D), axis=0))
    scaled_grad = normed_grad * gain
    token_grad = grad_f + scale * scaled_grad - scale ** 3 * values * lax.optimization_barrier(jnp.mean(scaled_grad * values, axis=-1, keepdims=True))
    return (token_grad.astype(jnp.bfloat16), gate_grad, up_grad, down_grad, router_grad, gain_grad)

def reference(inputs, cotangent, norm_gain, w_router, w_gate, w_up, w_down, routes):
    blocks = MICRO * N_DP * N_EXPERT
    picks = routes.reshape(LAYERS, blocks, TOK_MB, TOP)
    tokens = inputs.reshape(blocks, TOK_MB, D)
    saved = []
    for layer in range(LAYERS):
        saved.append(tokens)
        tokens = layer_forward(tokens, picks[layer], norm_gain[layer], w_router[layer], w_gate[layer], w_up[layer], w_down[layer])
    grad = cotangent.reshape(blocks, TOK_MB, D)
    results = [None] * LAYERS
    for layer in reversed(range(LAYERS)):
        grad, gate_grad, up_grad, down_grad, router_grad, gain_grad = layer_backward(grad, saved[layer], picks[layer], norm_gain[layer], w_router[layer], w_gate[layer], w_up[layer], w_down[layer])
        results[layer] = (gate_grad, up_grad, down_grad, router_grad, gain_grad)
    return (jnp.stack([item[0] for item in results]), jnp.stack([item[1] for item in results]), jnp.stack([item[2] for item in results]), jnp.stack([item[3] for item in results]), jnp.stack([item[4] for item in results]))
```

```python
import jax
import jax.numpy as jnp
import numpy as np
from jax import lax
from jax.experimental import pallas as pl
from jax.experimental.pallas import tpu as pltpu
from jax.sharding import PartitionSpec as P

EPS = 1e-05
BF = jnp.bfloat16
F32 = jnp.float32

ROWS = 32
CAP = 10
HALF = 2
TOK = ROWS * HALF
EXP = 32
USED = CAP * HALF
SLOT = 24
ALL = EXP * SLOT
LANE = 128


def constants():
    s = np.arange(ALL)
    of_expert, of_slot = s // SLOT, s % SLOT
    expand = (of_expert[None, :] == np.arange(EXP)[:, None]).astype(np.float32)
    place = (of_slot[:, None] == np.arange(LANE)[None, :]).astype(np.float32)
    place[of_slot >= USED] = 0
    slot_row = of_slot[None, :].astype(np.float32)
    t = np.arange(TOK)
    earlier = ((t[None, :] < t[:, None]) & (t[None, :] // ROWS == t[:, None] // ROWS)).astype(np.float32)
    start = (t // ROWS * CAP)[:, None].astype(np.float32)
    extra = [expand * (of_slot == USED + i)[None, :] for i in range(3)]
    return dict(
        expand=jnp.asarray(expand, BF),
        expand_t=jnp.asarray(expand.T, BF),
        place=jnp.asarray(place, BF),
        slot_row=jnp.asarray(slot_row, F32),
        earlier=jnp.asarray(earlier, BF),
        start=jnp.asarray(start, F32),
        extra=jnp.asarray(np.concatenate(extra, 0), BF),
        extra_t=jnp.asarray(np.stack([x.T for x in extra]), BF),
    )


def dot(a, b):
    return lax.dot_general(a, b, (((1,), (0,)), ((), ())), preferred_element_type=F32)


def dot_t0(a, b):
    return lax.dot_general(a, b, (((0,), (0,)), ((), ())), preferred_element_type=F32)


def dot_t1(a, b):
    return lax.dot_general(a, b, (((1,), (1,)), ((), ())), preferred_element_type=F32)


def split2(v):
    hi = v.astype(BF)
    return hi, (v - hi.astype(F32)).astype(BF)


def split3(v):
    hi = v.astype(BF)
    rest = v - hi.astype(F32)
    mid = rest.astype(BF)
    return hi, mid, (rest - mid.astype(F32)).astype(BF)


def slots_of(picks, c):
    columns = lax.broadcasted_iota(jnp.int32, (TOK, EXP), 1)
    mask = jnp.zeros((TOK, EXP), F32)
    for k in range(picks.shape[1]):
        mask = mask + jnp.where(picks[:, k : k + 1] == columns, 1.0, 0.0)
    rank = dot(c["earlier"], mask.astype(BF))
    slot = mask * (rank + c["start"] + 1.0) - 1.0
    table = dot(slot.astype(BF), c["expand"]) == c["slot_row"]
    return mask, table


def one(table):
    return jnp.where(table, 1.0, 0.0).astype(BF)


def norm(tokens, gain):
    values = tokens.astype(F32)
    scale = lax.rsqrt(jnp.mean(values * values, axis=-1, keepdims=True) + EPS)
    return (values * scale * gain).astype(BF), scale, values


def mix(normed, router, mask):
    logits = dot(normed, router)
    expo = jnp.where(mask > 0.0, jnp.exp(jnp.where(mask > 0.0, logits, 0.0)), 0.0)
    return expo / jnp.sum(expo, axis=-1, keepdims=True)


def weighted(table, parts, c):
    return [jnp.where(table, dot(v, c["expand"]), 0.0) for v in parts]


def small_rows(masked, c):
    row = jnp.sum(masked, axis=0, keepdims=True)
    return dot((c["expand"].astype(F32) * row).astype(BF), c["place"])


def spread_rows(smalls, c):
    total = None
    for i, v in enumerate(smalls):
        part = dot(c["extra_t"][i], v.astype(BF))
        total = part if total is None else total + part
    return total


def column_of(sent, index, c):
    row = dot(c["extra"][index * EXP : (index + 1) * EXP, :], sent[:, :LANE])
    wide = dot(c["expand_t"], row.astype(BF))
    return jnp.sum(wide * c["place"].astype(F32), axis=1, keepdims=True)


def with_small(rows, smalls, c):
    first = (rows[:, :LANE] + spread_rows(smalls, c)).astype(BF)
    return first, rows[:, LANE:].astype(BF)


CONST_NAMES = ("expand", "expand_t", "place", "slot_row", "earlier", "start", "extra", "extra_t")


def run(body, name, outs, args, consts, flops):
    consts = [consts[k] for k in CONST_NAMES]
    n = len(args)

    def kernel(*refs):
        values = [r for r in refs[:n]]
        c = {k: r[...] for k, r in zip(CONST_NAMES, refs[n : n + len(consts)])}
        body(c, values, refs[n + len(consts) :])

    size = sum(int(np.prod(a.shape)) * a.dtype.itemsize for a in args)
    return pl.pallas_call(
        kernel,
        out_shape=[jax.ShapeDtypeStruct(s, d) for s, d in outs],
        in_specs=[pl.BlockSpec(memory_space=pltpu.VMEM)] * (n + len(consts)),
        out_specs=[pl.BlockSpec(memory_space=pltpu.VMEM)] * len(outs),
        name=name,
        cost_estimate=pl.CostEstimate(flops=flops, bytes_accessed=size, transcendentals=0),
        compiler_params=pltpu.CompilerParams(vmem_limit_bytes=48 << 20),
    )(*args, *consts)


def start_body(c, ins, outs):
    tokens, picks, gain, router = ins
    send, weights = outs
    mask, table = slots_of(picks[...], c)
    normed, scale, values = norm(tokens[...], gain[...])
    weights[...] = mix(normed, router[...], mask)
    send[...] = dot_t0(one(table), normed).astype(BF)


def cotangent_body(c, ins, outs):
    grad, picks = ins
    (send,) = outs
    mask, table = slots_of(picks[...], c)
    send[...] = dot_t0(one(table), grad[...]).astype(BF)


def middle_body(c, ins, outs):
    tokens, picks0, weights0, returned, picks1, gain1, router1 = ins
    mixed_out, send, weights1 = outs
    mask0, table0 = slots_of(picks0[...], c)
    hi, lo = weighted(table0, split2(weights0[...]), c)
    back = returned[...]
    mixed = tokens[...].astype(F32) + dot(hi.astype(BF), back) + dot(lo.astype(BF), back)
    mixed = mixed.astype(BF)
    mixed_out[...] = mixed
    mask1, table1 = slots_of(picks1[...], c)
    normed, scale, values = norm(mixed, gain1[...])
    weights = mix(normed, router1[...], mask1)
    weights1[...] = weights
    rows = dot_t0(one(table1), normed)
    smalls = [small_rows(v, c) for v in weighted(table1, split2(weights), c)]
    send[:, :LANE], send[:, LANE:] = with_small(rows, smalls, c)


def turn_body(c, ins, outs):
    (tokens1, picks1, weights1, returned1, gain1, router1, grad, tokens0, picks0, weights0, returned0, gain0, router0) = ins
    send, gains = outs
    mask1, table1 = slots_of(picks1[...], c)
    back1 = returned1[...]
    pick1 = one(table1)
    expert_part = dot(pick1, back1)
    w1 = weights1[...]
    wg1 = jnp.zeros((TOK, EXP), F32)
    for i in range(3):
        column = column_of(back1, i, c)
        wg1 = wg1 + dot(pick1, (column * c["expand_t"].astype(F32)).astype(BF))
    lg1 = (w1 * (wg1 - jnp.sum(w1 * wg1, axis=-1, keepdims=True))).astype(BF)
    normed1, scale1, values1 = norm(tokens1[...], gain1[...])
    normed_grad1 = dot_t1(lg1, router1[...]) + expert_part
    gains[0:1, :] = jnp.sum(normed_grad1 * values1 * scale1, axis=0, keepdims=True)
    q = normed_grad1 * gain1[...]
    grad_f = grad[...].astype(F32)
    g0 = (
        grad_f + scale1 * q - scale1 * scale1 * scale1 * values1 * jnp.mean(q * values1, axis=-1, keepdims=True)
    ).astype(BF)
    mask0, table0 = slots_of(picks0[...], c)
    w0 = weights0[...]
    met = jnp.where(table0, dot_t1(g0, returned0[...]), 0.0)
    wg0 = jnp.zeros((TOK, EXP), F32)
    for part in split3(met):
        wg0 = wg0 + dot(part, c["expand_t"])
    lg0 = (w0 * (wg0 - jnp.sum(w0 * wg0, axis=-1, keepdims=True))).astype(BF)
    normed0, scale0, values0 = norm(tokens0[...], gain0[...])
    gains[1:2, :] = jnp.sum(dot_t1(lg0, router0[...]) * values0 * scale0, axis=0, keepdims=True)
    hi, lo = weighted(table0, split2(w0), c)
    rows = dot_t0(hi.astype(BF), g0) + dot_t0(lo.astype(BF), g0)
    smalls = [small_rows(weighted(table0, [lg0], c)[0], c), small_rows(weighted(table1, [lg1], c)[0], c)]
    send[:, :LANE], send[:, LANE:] = with_small(rows, smalls, c)


def exchanged(rows):
    return lax.all_to_all(rows, "expert", split_axis=0, concat_axis=0, tiled=True)


def swapped(value):
    return lax.ppermute(value, "pipe", [(0, 1), (1, 0)])


def blocks_of(gate, up, down):
    half = gate.shape[0] // 2
    quarter = half // 2
    rows = []
    for d in range(2):
        for p in range(2):
            at = d * half + p * quarter
            rows.append(
                jnp.concatenate(
                    [
                        gate[at : at + quarter],
                        up[at : at + quarter],
                        down[p * quarter : (p + 1) * quarter, d * half : (d + 1) * half],
                    ],
                    axis=0,
                )
            )
    return jnp.stack(rows).reshape(2, 2, 3 * quarter, half).astype(BF)


def shards(inputs, cotangent, norm_gain, w_router, w_gate, w_up, w_down, routes):
    c = constants()
    pipe = lax.axis_index("pipe")
    data = lax.axis_index("dp")
    width = inputs.shape[-1]
    first = pipe == 0

    def own_part(v):
        return lax.dynamic_slice_in_dim(v, pipe * HALF, HALF, 0).reshape(TOK, -1)

    def other_part(v):
        return lax.dynamic_slice_in_dim(v, (1 - pipe) * HALF, HALF, 0).reshape(TOK, -1)

    def both(own, other):
        return jnp.where(first, own, other), jnp.where(first, other, own)

    picks0, picks1 = both(own_part(routes[0]), swapped(other_part(routes[0])))
    gain0, gain1 = both(norm_gain, swapped(norm_gain))
    router0, router1 = both(w_router[0], swapped(w_router[0]))
    gate0, gate1 = both(w_gate[0, 0], swapped(w_gate[0, 0]))
    up0, up1 = both(w_up[0, 0], swapped(w_up[0, 0]))
    down0, down1 = both(w_down[0, 0], swapped(w_down[0, 0]))
    tokens0 = own_part(inputs)
    grad1 = own_part(cotangent)

    rows_shape = ((ALL, width), BF)
    send0, weights0 = run(
        start_body, "start", [rows_shape, ((TOK, EXP), F32)], [tokens0, picks0, gain0, router0], c, 100_000_000
    )
    recv0 = exchanged(send0)
    (send_g,) = run(cotangent_body, "cotangent", [rows_shape], [grad1, picks1], c, 100_000_000)
    grad_rows = exchanged(send_g)

    gate_act0 = dot(recv0, gate0)
    up_act0 = dot(recv0, up0)
    hidden0 = (jax.nn.silu(gate_act0) * up_act0).astype(BF)
    returned0 = exchanged(dot(hidden0, down0).astype(BF))

    tokens1, send1, weights1 = run(
        middle_body,
        "middle",
        [((TOK, width), BF), rows_shape, ((TOK, EXP), F32)],
        [tokens0, picks0, weights0, returned0, picks1, gain1, router1],
        c,
        300_000_000,
    )
    recv1 = exchanged(send1)

    def backward(rows_in, gate_act, up_act, hidden, scaled, gate_mat, up_mat, down_mat):
        grad_hidden = dot_t1(scaled, down_mat)
        sig = jax.nn.sigmoid(gate_act)
        gate_back = (grad_hidden * up_act * sig * (1.0 + gate_act * (1.0 - sig))).astype(BF)
        up_back = (grad_hidden * gate_act * sig).astype(BF)
        back = (dot_t1(gate_back, gate_mat) + dot_t1(up_back, up_mat)).astype(BF)
        parts = blocks_of(dot_t0(rows_in, gate_back), dot_t0(rows_in, up_back), dot_t0(hidden, scaled))
        return back, parts

    gate_act1 = dot(recv1, gate1)
    up_act1 = dot(recv1, up1)
    hidden1 = (jax.nn.silu(gate_act1) * up_act1).astype(BF)
    out1 = dot(hidden1, down1).astype(BF)
    grad_rows_f = grad_rows.astype(F32)
    wg_column = jnp.sum(grad_rows_f * out1.astype(F32), axis=1, keepdims=True)
    w_column = column_of(recv1, 0, c) + column_of(recv1, 1, c)
    scaled1 = (w_column * grad_rows_f).astype(BF)
    back1, parts1 = backward(recv1, gate_act1, up_act1, hidden1, scaled1, gate1, up1, down1)

    def pack_body(c, ins, outs):
        back, column = ins
        (send,) = outs
        smalls = [
            dot(c["expand"], (part.astype(F32) * c["place"].astype(F32)).astype(BF)) for part in split3(column[...])
        ]
        send[:, :LANE] = (back[:, :LANE].astype(F32) + spread_rows(smalls, c)).astype(BF)
        send[:, LANE:] = back[:, LANE:]

    (send_b,) = run(pack_body, "pack", [rows_shape], [back1, wg_column], c, 100_000_000)
    returned1 = exchanged(send_b)

    def over_groups(parts):
        kept = lax.dynamic_index_in_dim(parts, pipe, 1, keepdims=False)
        sent = lax.dynamic_index_in_dim(parts, 1 - pipe, 1, keepdims=False)
        paired = (kept.astype(F32) + swapped(sent).astype(F32)).astype(BF)
        kept = lax.dynamic_index_in_dim(paired, data, 0, keepdims=False)
        sent = lax.dynamic_index_in_dim(paired, 1 - data, 0, keepdims=False)
        got = lax.ppermute(sent, "dp", [(0, 1), (1, 0)])
        return (kept.astype(F32) + got.astype(F32)).astype(BF)

    summed1 = over_groups(parts1)

    send2, gains = run(
        turn_body,
        "turn",
        [rows_shape, ((2, width), F32)],
        [tokens1, picks1, weights1, returned1, gain1, router1, grad1, tokens0, picks0, weights0, returned0, gain0, router0],
        c,
        600_000_000,
    )
    recv2 = exchanged(send2)
    back0, parts0 = backward(recv0, gate_act0, up_act0, hidden0, recv2, gate0, up0, down0)
    lg0 = column_of(recv2, 0, c)
    lg1 = column_of(recv2, 1, c)
    recv0_f = recv0.astype(F32)
    gain_rows = jnp.sum(recv0_f * back0.astype(F32), axis=0, keepdims=True) / gain0
    column0 = jnp.sum(recv0_f * lg0, axis=0, keepdims=True)
    column1 = jnp.sum(recv1.astype(F32) * lg1, axis=0, keepdims=True)
    small0 = jnp.concatenate([column0, gain_rows + gains[1:2]], axis=0)
    small1 = jnp.concatenate([column1, gains[0:1]], axis=0)
    mine, theirs = both(small0, small1)
    mine = mine + swapped(theirs)
    group = 2 * EXP
    told = jnp.broadcast_to(mine.reshape(1, 2 * width // LANE, LANE), (group, 2 * width // LANE, LANE))
    heard = lax.all_to_all(told, ("dp", "expert"), split_axis=0, concat_axis=0, tiled=True)
    heard = heard.reshape(2, EXP, 2, width)
    router_sum = (heard[0, :, 0] + heard[1, :, 0]).T
    gain_sum = jnp.sum(heard[:, :, 1], axis=(0, 1))

    summed0 = over_groups(parts0)
    mine, theirs = both(summed0, summed1)
    got = swapped(theirs)
    low, high = both(mine, got)
    quarter = low.shape[0] // 3
    outs = [
        jnp.concatenate([low[i * quarter : (i + 1) * quarter], high[i * quarter : (i + 1) * quarter]], axis=0)
        for i in range(3)
    ]
    return (
        outs[0][None, None],
        outs[1][None, None],
        outs[2][None, None],
        router_sum[None],
        gain_sum[None],
    )


def solution(mesh):
    in_specs = (
        P(None, ("dp", "expert"), None),
        P(None, ("dp", "expert"), None),
        P("pipe", None),
        P("pipe", None, None),
        P("pipe", "expert", None, None),
        P("pipe", "expert", None, None),
        P("pipe", "expert", None, None),
        P("pipe", None, ("dp", "expert"), None),
    )
    out_specs = (
        P("pipe", "expert", "dp", None),
        P("pipe", "expert", "dp", None),
        P("pipe", "expert", None, "dp"),
        P("pipe", None, None),
        P("pipe", None),
    )
    return jax.shard_map(shards, mesh=mesh, in_specs=in_specs, out_specs=out_specs, check_vma=False)
```

```python
import jax
import jax.numpy as jnp
import numpy as np
from jax import lax
from jax.experimental import pallas as pl
from jax.experimental.pallas import tpu as pltpu
from jax.sharding import PartitionSpec as P

EPS = 1e-05
BF = jnp.bfloat16
F32 = jnp.float32

ROWS = 32
CAP = 10
HALF = 2
TOK = ROWS * HALF
EXP = 32
USED = CAP * HALF
SLOT = 24
ALL = EXP * SLOT
LANE = 128


class Tables:
    def __init__(self, n):
        self.n, self.rows, self.made = n, n * SLOT, {}

    def get(self, name, make):
        if name not in self.made:
            self.made[name] = make()
        return self.made[name]

    def place_of(self, shape, axis):
        s = lax.broadcasted_iota(jnp.int32, shape, axis).astype(F32)
        expert = jnp.floor((s + 0.5) * (1.0 / SLOT))
        return expert, s - SLOT * expert

    def flags(self, test):
        return jnp.where(test, 1.0, 0.0)

    @property
    def expand(self):
        def make():
            shape = (self.n, self.rows)
            expert, slot = self.place_of(shape, 1)
            return self.flags(expert == lax.broadcasted_iota(jnp.int32, shape, 0).astype(F32))

        return self.get("expand", make)

    @property
    def expand_t(self):
        def make():
            shape = (self.rows, self.n)
            expert, slot = self.place_of(shape, 0)
            return self.flags(expert == lax.broadcasted_iota(jnp.int32, shape, 1).astype(F32))

        return self.get("expand_t", make)

    @property
    def slot_row(self):
        return self.get("slot_row", lambda: self.place_of((1, self.rows), 1)[1])

    @property
    def slot_column(self):
        return self.get("slot_column", lambda: self.place_of((self.rows, 1), 0)[1])

    @property
    def place(self):
        def make():
            shape = (self.rows, LANE)
            slot = self.place_of(shape, 0)[1]
            lane = lax.broadcasted_iota(jnp.int32, shape, 1).astype(F32)
            return self.flags((slot == lane) & (slot < USED))

        return self.get("place", make)

    def extra(self, i):
        return self.get(("extra", i), lambda: jnp.where(self.slot_row == USED + i, self.expand, 0.0).astype(BF))

    def extra_t(self, i):
        return self.get(("extra_t", i), lambda: jnp.where(self.slot_column == USED + i, self.expand_t, 0.0).astype(BF))


def dot(a, b):
    return lax.dot_general(a, b, (((1,), (0,)), ((), ())), preferred_element_type=F32)


def dot_t0(a, b):
    return lax.dot_general(a, b, (((0,), (0,)), ((), ())), preferred_element_type=F32)


def dot_t1(a, b):
    return lax.dot_general(a, b, (((1,), (1,)), ((), ())), preferred_element_type=F32)


def split2(v):
    hi = v.astype(BF)
    return hi, (v - hi.astype(F32)).astype(BF)


def split3(v):
    hi = v.astype(BF)
    rest = v - hi.astype(F32)
    mid = rest.astype(BF)
    return hi, mid, (rest - mid.astype(F32)).astype(BF)


def slots_of(picks, c):
    columns = lax.broadcasted_iota(jnp.int32, (TOK, EXP), 1)
    mask = jnp.zeros((TOK, EXP), F32)
    for k in range(picks.shape[1]):
        mask = mask + jnp.where(picks[:, k : k + 1] == columns, 1.0, 0.0)
    row = lax.broadcasted_iota(jnp.int32, (TOK, TOK), 0)
    column = lax.broadcasted_iota(jnp.int32, (TOK, TOK), 1)
    earlier = jnp.where((column < row) & ((row < ROWS) | (column >= ROWS)), 1.0, 0.0).astype(BF)
    start = jnp.where(lax.broadcasted_iota(jnp.int32, (TOK, EXP), 0) < ROWS, 0.0, 1.0 * CAP)
    slot = mask * (dot(earlier, mask.astype(BF)) + start + 1.0) - 1.0
    table = dot(slot.astype(BF), c.expand.astype(BF)) == c.slot_row
    return mask, table


def one(table):
    return jnp.where(table, 1.0, 0.0).astype(BF)


def norm(tokens, gain):
    values = tokens.astype(F32)
    scale = lax.rsqrt(jnp.mean(values * values, axis=-1, keepdims=True) + EPS)
    return (values * scale * gain).astype(BF), scale, values


def mix(normed, router, mask):
    logits = dot(normed, router)
    expo = jnp.where(mask > 0.0, jnp.exp(jnp.where(mask > 0.0, logits, 0.0)), 0.0)
    return expo / jnp.sum(expo, axis=-1, keepdims=True)


def weighted(table, parts, c):
    return [jnp.where(table, dot(v, c.expand.astype(BF)), 0.0) for v in parts]


def small_rows(masked, c):
    row = jnp.sum(masked, axis=0, keepdims=True)
    return dot((c.expand * row).astype(BF), c.place.astype(BF))


def small_columns(column, c):
    return dot(c.expand.astype(BF), (column.astype(F32) * c.place).astype(BF))


def spread_rows(smalls, c):
    total = None
    for i, v in enumerate(smalls):
        part = dot(c.extra_t(i), v.astype(BF))
        total = part if total is None else total + part
    return total


def column_of(first, index, c):
    wide = dot(c.expand_t.astype(BF), dot(c.extra(index), first).astype(BF))
    return jnp.sum(wide * c.place, axis=1, keepdims=True)


def with_small(rows, smalls, c):
    first = (rows[:, :LANE] + spread_rows(smalls, c)).astype(BF)
    return first, rows[:, LANE:].astype(BF)


def params(limit=40):
    return pltpu.CompilerParams(vmem_limit_bytes=limit << 20)


def cost(flops, arrays):
    size = sum(int(np.prod(a.shape)) * jnp.dtype(a.dtype).itemsize for a in arrays)
    return pl.CostEstimate(flops=flops, bytes_accessed=size, transcendentals=0)


def run(body, name, outs, args, flops):
    n = len(args)

    def kernel(*refs):
        body(Tables(EXP), refs[:n], refs[n:])

    out_shape = [jax.ShapeDtypeStruct(s, d) for s, d in outs]
    return pl.pallas_call(
        kernel,
        out_shape=out_shape,
        in_specs=[pl.BlockSpec(memory_space=pltpu.VMEM)] * n,
        out_specs=[pl.BlockSpec(memory_space=pltpu.VMEM)] * len(outs),
        name=name,
        cost_estimate=cost(flops, list(args) + out_shape),
        compiler_params=params(),
    )(*args)


PART = 16


def whole(a):
    return pl.BlockSpec(a.shape, lambda i: (0,) * len(a.shape))


def rows_block(width):
    return pl.BlockSpec((PART * SLOT, width), lambda i: (i, 0))


def forward_expert(recv, gate_mat, up_mat, down_mat, name):
    width, inner = gate_mat.shape

    def kernel(x, wg, wu, wd, out, fa, fb, hid):
        rows = x[...]
        gate = dot(rows, wg[...])
        up = dot(rows, wu[...])
        sig = jax.nn.sigmoid(gate)
        act = gate * sig
        hidden = (act * up).astype(BF)
        out[...] = dot(hidden, wd[...]).astype(BF)
        hid[...] = hidden
        fb[...] = act
        fa[...] = up * sig * (1.0 + gate * (1.0 - sig))

    out_shape = [
        jax.ShapeDtypeStruct((ALL, width), BF),
        jax.ShapeDtypeStruct((ALL, inner), F32),
        jax.ShapeDtypeStruct((ALL, inner), F32),
        jax.ShapeDtypeStruct((ALL, inner), BF),
    ]
    args = [recv, gate_mat, up_mat, down_mat]
    return pl.pallas_call(
        kernel,
        grid=(EXP // PART,),
        out_shape=out_shape,
        in_specs=[rows_block(width), whole(gate_mat), whole(up_mat), whole(down_mat)],
        out_specs=[rows_block(width), rows_block(inner), rows_block(inner), rows_block(inner)],
        name=name,
        cost_estimate=cost(6 * ALL * width * inner, args + out_shape),
        compiler_params=params(),
    )(*args)


def backward_expert(recv, grads, out, fa, fb, gate_mat, up_mat, down_mat):
    width, inner = gate_mat.shape

    def kernel(x, g, o, fa, fb, wg, wu, wd, send, scaled_out, gate_out, up_out):
        c = Tables(PART)
        first = x[...]
        weight = column_of(first, 0, c) + column_of(first, 1, c)
        grad = g[...].astype(F32)
        weight_grad = jnp.sum(grad * o[...].astype(F32), axis=1, keepdims=True)
        scaled = (weight * grad).astype(BF)
        scaled_out[...] = scaled
        grad_hidden = dot_t1(scaled, wd[...])
        gate_back = (grad_hidden * fa[...]).astype(BF)
        up_back = (grad_hidden * fb[...]).astype(BF)
        gate_out[...] = gate_back
        up_out[...] = up_back
        back = dot_t1(gate_back, wg[...]) + dot_t1(up_back, wu[...])
        smalls = [small_columns(part, c) for part in split3(weight_grad)]
        send[:, :LANE], send[:, LANE:] = with_small(back, smalls, c)

    out_shape = [
        jax.ShapeDtypeStruct((ALL, width), BF),
        jax.ShapeDtypeStruct((ALL, width), BF),
        jax.ShapeDtypeStruct((ALL, inner), BF),
        jax.ShapeDtypeStruct((ALL, inner), BF),
    ]
    args = [recv, grads, out, fa, fb, gate_mat, up_mat, down_mat]
    return pl.pallas_call(
        kernel,
        grid=(EXP // PART,),
        out_shape=out_shape,
        in_specs=[rows_block(LANE), rows_block(width), rows_block(width), rows_block(inner), rows_block(inner)]
        + [whole(gate_mat), whole(up_mat), whole(down_mat)],
        out_specs=[rows_block(width), rows_block(width), rows_block(inner), rows_block(inner)],
        name="backward1",
        cost_estimate=cost(6 * ALL * width * inner, args + out_shape),
        compiler_params=params(),
    )(*args)


def weight_blocks(at, near, gate_back, up_back, left, scaled, hidden, name):
    width, inner = left.shape[1], hidden.shape[1]
    half, quarter = width // 2, width // 4

    def kernel(at, gb, ub, x, sc, hid, out):
        step = pl.program_id(0)
        pipe, data = at[0], at[1]
        which = jnp.where(step == 0, 1 - pipe, pipe)
        group = data if near else 1 - data
        rows = x[:, pl.ds(pl.multiple_of(group * half + which * quarter, quarter), quarter)]
        out[0, 0:quarter, :] = dot_t0(rows, gb[...]).astype(BF)
        out[0, quarter : 2 * quarter, :] = dot_t0(rows, ub[...]).astype(BF)
        low = hid[:, pl.ds(pl.multiple_of(which * quarter, quarter), quarter)]
        wide = sc[:, pl.ds(pl.multiple_of(group * half, half), half)]
        out[0, 2 * quarter :, :] = dot_t0(low, wide).astype(BF)

    out_shape = jax.ShapeDtypeStruct((2, 3 * quarter, half), BF)
    args = [gate_back, up_back, left, scaled, hidden]
    return pl.pallas_call(
        kernel,
        grid=(2,),
        out_shape=out_shape,
        in_specs=[pl.BlockSpec(memory_space=pltpu.SMEM)] + [whole(v) for v in args],
        out_specs=pl.BlockSpec((1, 3 * quarter, half), lambda i: (i, 0, 0)),
        name=name,
        cost_estimate=cost(3 * ALL * width * inner, args + [out_shape]),
        compiler_params=params(),
    )(at, *args)


def backward_first(recv, fa, fb, down_mat):
    inner = down_mat.shape[0]
    width = down_mat.shape[1]

    def kernel(x, fa, fb, wd, gate_out, up_out):
        grad_hidden = dot_t1(x[...], wd[...])
        gate_out[...] = (grad_hidden * fa[...]).astype(BF)
        up_out[...] = (grad_hidden * fb[...]).astype(BF)

    out_shape = [jax.ShapeDtypeStruct((ALL, inner), BF)] * 2
    args = [recv, fa, fb, down_mat]
    return pl.pallas_call(
        kernel,
        grid=(EXP // PART,),
        out_shape=out_shape,
        in_specs=[rows_block(width), rows_block(inner), rows_block(inner), whole(down_mat)],
        out_specs=[rows_block(inner), rows_block(inner)],
        name="backward0",
        cost_estimate=cost(2 * ALL * width * inner, args + out_shape),
        compiler_params=params(),
    )(*args)


def rest(at, recv0, recv1, recv2, gate_back, up_back, gate_mat, up_mat, gain, gains):
    width, inner = gate_mat.shape
    steps = EXP // PART

    def kernel(at, x0, x1, x2, gb, ub, wg, wu, gain, gains, out, total):
        step = pl.program_id(0)
        c = Tables(PART)

        @pl.when(step == 0)
        def _():
            total[...] = jnp.zeros_like(total)

        first = x2[...]
        back = (dot_t1(gb[...], wg[...]) + dot_t1(ub[...], wu[...])).astype(BF).astype(F32)
        rows0 = x0[...].astype(F32)
        total[0:1, :] += jnp.sum(rows0 * column_of(first, 0, c), axis=0, keepdims=True)
        total[1:2, :] += jnp.sum(rows0 * back, axis=0, keepdims=True)
        total[2:3, :] += jnp.sum(x1[...].astype(F32) * column_of(first, 1, c), axis=0, keepdims=True)

        @pl.when(step == steps - 1)
        def _():
            gain0 = total[1:2, :] / gain[...] + gains[1:2, :]
            gain1 = gains[0:1, :]
            mine = at[0] == 0
            column0, column1 = total[0:1, :], total[2:3, :]
            out[0:1, :] = jnp.where(mine, column0, column1)
            out[1:2, :] = jnp.where(mine, gain0, gain1)
            out[2:3, :] = jnp.where(mine, column1, column0)
            out[3:4, :] = jnp.where(mine, gain1, gain0)

    out_shape = jax.ShapeDtypeStruct((4, width), F32)
    args = [recv0, recv1, recv2, gate_back, up_back, gate_mat, up_mat, gain, gains]
    return pl.pallas_call(
        kernel,
        grid=(steps,),
        out_shape=out_shape,
        in_specs=[pl.BlockSpec(memory_space=pltpu.SMEM), rows_block(width), rows_block(width), rows_block(LANE)]
        + [rows_block(inner), rows_block(inner), whole(gate_mat), whole(up_mat), whole(gain), whole(gains)],
        out_specs=whole(out_shape),
        scratch_shapes=[pltpu.VMEM((8, width), F32)],
        name="rest",
        cost_estimate=cost(4 * ALL * width * inner, args),
        compiler_params=params(),
    )(at, *args)


def start_body(c, ins, outs):
    tokens, picks, gain, router = ins
    send, weights = outs
    mask, table = slots_of(picks[...], c)
    normed, scale, values = norm(tokens[...], gain[...])
    weights[...] = mix(normed, router[...], mask)
    send[...] = dot_t0(one(table), normed).astype(BF)


def cotangent_body(c, ins, outs):
    grad, picks = ins
    (send,) = outs
    mask, table = slots_of(picks[...], c)
    send[...] = dot_t0(one(table), grad[...]).astype(BF)


def middle_body(c, ins, outs):
    tokens, picks0, weights0, returned, picks1, gain1, router1 = ins
    mixed_out, send, weights1 = outs
    mask0, table0 = slots_of(picks0[...], c)
    hi, lo = weighted(table0, split2(weights0[...]), c)
    back = returned[...]
    mixed = tokens[...].astype(F32) + dot(hi.astype(BF), back) + dot(lo.astype(BF), back)
    mixed = mixed.astype(BF)
    mixed_out[...] = mixed
    mask1, table1 = slots_of(picks1[...], c)
    normed, scale, values = norm(mixed, gain1[...])
    weights = mix(normed, router1[...], mask1)
    weights1[...] = weights
    rows = dot_t0(one(table1), normed)
    smalls = [small_rows(v, c) for v in weighted(table1, split2(weights), c)]
    send[:, :LANE], send[:, LANE:] = with_small(rows, smalls, c)


def turn_body(c, ins, outs):
    (tokens1, picks1, weights1, returned1, gain1, router1, grad, tokens0, picks0, weights0, returned0, gain0, router0) = ins
    send, gains = outs
    mask1, table1 = slots_of(picks1[...], c)
    back1 = returned1[...]
    pick1 = one(table1)
    expert_part = dot(pick1, back1)
    w1 = weights1[...]
    wg1 = jnp.zeros((TOK, EXP), F32)
    for i in range(3):
        column = column_of(back1[:, :LANE], i, c)
        wg1 = wg1 + dot(pick1, (column * c.expand_t).astype(BF))
    lg1 = (w1 * (wg1 - jnp.sum(w1 * wg1, axis=-1, keepdims=True))).astype(BF)
    normed1, scale1, values1 = norm(tokens1[...], gain1[...])
    normed_grad1 = dot_t1(lg1, router1[...]) + expert_part
    gains[0:1, :] = jnp.sum(normed_grad1 * values1 * scale1, axis=0, keepdims=True)
    q = normed_grad1 * gain1[...]
    grad_f = grad[...].astype(F32)
    g0 = (
        grad_f + scale1 * q - scale1 * scale1 * scale1 * values1 * jnp.mean(q * values1, axis=-1, keepdims=True)
    ).astype(BF)
    mask0, table0 = slots_of(picks0[...], c)
    w0 = weights0[...]
    met = jnp.where(table0, dot_t1(g0, returned0[...]), 0.0)
    wg0 = jnp.zeros((TOK, EXP), F32)
    for part in split3(met):
        wg0 = wg0 + dot(part, c.expand_t.astype(BF))
    lg0 = (w0 * (wg0 - jnp.sum(w0 * wg0, axis=-1, keepdims=True))).astype(BF)
    normed0, scale0, values0 = norm(tokens0[...], gain0[...])
    gains[1:2, :] = jnp.sum(dot_t1(lg0, router0[...]) * values0 * scale0, axis=0, keepdims=True)
    hi, lo = weighted(table0, split2(w0), c)
    rows = dot_t0(hi.astype(BF), g0) + dot_t0(lo.astype(BF), g0)
    smalls = [small_rows(weighted(table0, [lg0], c)[0], c), small_rows(weighted(table1, [lg1], c)[0], c)]
    send[:, :LANE], send[:, LANE:] = with_small(rows, smalls, c)


def exchanged(rows):
    return lax.all_to_all(rows, "expert", split_axis=0, concat_axis=0, tiled=True)


def swapped(value):
    return lax.ppermute(value, "pipe", [(0, 1), (1, 0)])


def shards(inputs, cotangent, norm_gain, w_router, w_gate, w_up, w_down, routes):
    pipe = lax.axis_index("pipe")
    data = lax.axis_index("dp")
    at = jnp.stack([pipe, data]).astype(jnp.int32)
    width = inputs.shape[-1]
    first = pipe == 0

    def own_part(v):
        return lax.dynamic_slice_in_dim(v, pipe * HALF, HALF, 0).reshape(TOK, -1)

    def other_part(v):
        return lax.dynamic_slice_in_dim(v, (1 - pipe) * HALF, HALF, 0).reshape(TOK, -1)

    def both(own, other):
        return jnp.where(first, own, other), jnp.where(first, other, own)

    picks0, picks1 = both(own_part(routes[0]), swapped(other_part(routes[0])))
    gain0, gain1 = both(norm_gain, swapped(norm_gain))
    router0, router1 = both(w_router[0], swapped(w_router[0]))
    tokens0 = own_part(inputs)
    grad1 = own_part(cotangent)

    rows_shape = ((ALL, width), BF)
    send0, weights0 = run(
        start_body, "start", [rows_shape, ((TOK, EXP), F32)], [tokens0, picks0, gain0, router0], 100_000_000
    )
    recv0 = exchanged(send0)
    mats = [both(w[0, 0], swapped(w[0, 0])) for w in (w_gate, w_up, w_down)]
    (gate0, gate1), (up0, up1), (down0, down1) = lax.optimization_barrier(mats)
    (send_g,) = run(cotangent_body, "cotangent", [rows_shape], [grad1, picks1], 100_000_000)
    grad_rows = exchanged(send_g)

    out0, fa0, fb0, hidden0 = forward_expert(recv0, gate0, up0, down0, "forward0")
    returned0 = exchanged(out0)

    tokens1, send1, weights1 = run(
        middle_body,
        "middle",
        [((TOK, width), BF), rows_shape, ((TOK, EXP), F32)],
        [tokens0, picks0, weights0, returned0, picks1, gain1, router1],
        300_000_000,
    )
    recv1 = exchanged(send1)

    out1, fa1, fb1, hidden1 = forward_expert(recv1, gate1, up1, down1, "forward1")
    send_b, scaled1, gate_back1, up_back1 = backward_expert(recv1, grad_rows, out1, fa1, fb1, gate1, up1, down1)
    returned1 = exchanged(send_b)

    def over_groups(args, name):
        far = weight_blocks(at, False, *args, name + "_far")
        far = (far[1].astype(F32) + swapped(far[0]).astype(F32)).astype(BF)
        got = lax.ppermute(far, "dp", [(0, 1), (1, 0)])
        near = weight_blocks(at, True, *args, name + "_near")
        near = near[1].astype(F32) + swapped(near[0]).astype(F32)
        return (near + got.astype(F32)).astype(BF)

    summed1 = over_groups([gate_back1, up_back1, recv1, scaled1, hidden1], "grads1")

    send2, gains = run(
        turn_body,
        "turn",
        [rows_shape, ((2, width), F32)],
        [tokens1, picks1, weights1, returned1, gain1, router1, grad1, tokens0, picks0, weights0, returned0, gain0, router0],
        600_000_000,
    )
    recv2 = exchanged(send2)
    gate_back0, up_back0 = backward_first(recv2, fa0, fb0, down0)
    summed0 = over_groups([gate_back0, up_back0, recv0, recv2, hidden0], "grads0")

    small = rest(at, recv0, recv1, recv2, gate_back0, up_back0, gate0, up0, gain0, gains)
    mine = small[0:2] + swapped(small[2:4])
    group = 2 * EXP
    told = jnp.broadcast_to(mine.reshape(1, 2 * width // LANE, LANE), (group, 2 * width // LANE, LANE))
    heard = lax.all_to_all(told, ("dp", "expert"), split_axis=0, concat_axis=0, tiled=True)
    heard = heard.reshape(2, EXP, 2, width)
    router_sum = (heard[0, :, 0] + heard[1, :, 0]).T
    gain_sum = jnp.sum(heard[:, :, 1], axis=(0, 1))

    mine, theirs = both(summed0, summed1)
    low, high = both(mine, swapped(theirs))
    quarter = low.shape[0] // 3
    outs = [
        jnp.concatenate([low[i * quarter : (i + 1) * quarter], high[i * quarter : (i + 1) * quarter]], axis=0)
        for i in range(3)
    ]
    return (
        outs[0][None, None],
        outs[1][None, None],
        outs[2][None, None],
        router_sum[None],
        gain_sum[None],
    )


def solution(mesh):
    in_specs = (
        P(None, ("dp", "expert"), None),
        P(None, ("dp", "expert"), None),
        P("pipe", None),
        P("pipe", None, None),
        P("pipe", "expert", None, None),
        P("pipe", "expert", None, None),
        P("pipe", "expert", None, None),
        P("pipe", None, ("dp", "expert"), None),
    )
    out_specs = (
        P("pipe", "expert", "dp", None),
        P("pipe", "expert", "dp", None),
        P("pipe", "expert", None, "dp"),
        P("pipe", None, None),
        P("pipe", None),
    )
    return jax.shard_map(shards, mesh=mesh, in_specs=in_specs, out_specs=out_specs, check_vma=False)
```

```python
import functools

import jax
import jax.numpy as jnp
import numpy as np
from jax import lax
from jax.experimental import pallas as pl
from jax.experimental.pallas import tpu as pltpu
from jax.sharding import PartitionSpec as P

EPS = 1e-05
BF = jnp.bfloat16
F32 = jnp.float32

ROWS = 32
CAP = 10
HALF = 2
TOK = ROWS * HALF
EXP = 32
USED = CAP * HALF
SLOT = 24
ALL = EXP * SLOT
LANE = 128


class Tables:
    def __init__(self, n, slots=SLOT):
        self.n, self.slots, self.rows, self.made = n, slots, n * slots, {}

    def get(self, name, make):
        if name not in self.made:
            self.made[name] = make()
        return self.made[name]

    def place_of(self, shape, axis):
        s = lax.broadcasted_iota(jnp.int32, shape, axis).astype(F32)
        expert = jnp.floor((s + 0.5) * (1.0 / self.slots))
        return expert, s - self.slots * expert

    def flags(self, test):
        return jnp.where(test, 1.0, 0.0)

    @property
    def expand(self):
        def make():
            shape = (self.n, self.rows)
            expert, slot = self.place_of(shape, 1)
            return self.flags(expert == lax.broadcasted_iota(jnp.int32, shape, 0).astype(F32))

        return self.get("expand", make)

    @property
    def expand_t(self):
        def make():
            shape = (self.rows, self.n)
            expert, slot = self.place_of(shape, 0)
            return self.flags(expert == lax.broadcasted_iota(jnp.int32, shape, 1).astype(F32))

        return self.get("expand_t", make)

    @property
    def slot_row(self):
        return self.get("slot_row", lambda: self.place_of((1, self.rows), 1)[1])

    @property
    def slot_column(self):
        return self.get("slot_column", lambda: self.place_of((self.rows, 1), 0)[1])

    @property
    def place(self):
        def make():
            shape = (self.rows, LANE)
            slot = self.place_of(shape, 0)[1]
            lane = lax.broadcasted_iota(jnp.int32, shape, 1).astype(F32)
            return self.flags((slot == lane) & (slot < USED))

        return self.get("place", make)

    def extra(self, i):
        return self.get(("extra", i), lambda: jnp.where(self.slot_row == USED + i, self.expand, 0.0).astype(BF))

    def extra_t(self, i):
        return self.get(("extra_t", i), lambda: jnp.where(self.slot_column == USED + i, self.expand_t, 0.0).astype(BF))


def dot(a, b):
    return lax.dot_general(a, b, (((1,), (0,)), ((), ())), preferred_element_type=F32)


def dot_t0(a, b):
    return lax.dot_general(a, b, (((0,), (0,)), ((), ())), preferred_element_type=F32)


def dot_t1(a, b):
    return lax.dot_general(a, b, (((1,), (1,)), ((), ())), preferred_element_type=F32)


def split2(v):
    hi = v.astype(BF)
    return hi, (v - hi.astype(F32)).astype(BF)


def split3(v):
    hi = v.astype(BF)
    rest = v - hi.astype(F32)
    mid = rest.astype(BF)
    return hi, mid, (rest - mid.astype(F32)).astype(BF)


def slots_of(picks, c, shift=0.0):
    columns = lax.broadcasted_iota(jnp.int32, (TOK, EXP), 1)
    mask = jnp.zeros((TOK, EXP), F32)
    for k in range(picks.shape[1]):
        mask = mask + jnp.where(picks[:, k : k + 1] == columns, 1.0, 0.0)
    row = lax.broadcasted_iota(jnp.int32, (TOK, TOK), 0)
    column = lax.broadcasted_iota(jnp.int32, (TOK, TOK), 1)
    earlier = jnp.where((column < row) & ((row < ROWS) | (column >= ROWS)), 1.0, 0.0).astype(BF)
    start = jnp.where(lax.broadcasted_iota(jnp.int32, (TOK, EXP), 0) < ROWS, 0.0, 1.0 * CAP)
    slot = mask * (dot(earlier, mask.astype(BF)) + start + 1.0 + shift) - 1.0
    table = dot(slot.astype(BF), c.expand.astype(BF)) == c.slot_row
    return mask, table


def one(table):
    return jnp.where(table, 1.0, 0.0).astype(BF)


def norm(tokens, gain):
    values = tokens.astype(F32)
    scale = lax.rsqrt(jnp.mean(values * values, axis=-1, keepdims=True) + EPS)
    return (values * scale * gain).astype(BF), scale, values


def mix(normed, router, mask):
    logits = dot_t1(normed, router)
    expo = jnp.where(mask > 0.0, jnp.exp(jnp.where(mask > 0.0, logits, 0.0)), 0.0)
    return expo / jnp.sum(expo, axis=-1, keepdims=True)


def weighted(table, parts, c):
    return [jnp.where(table, dot(v, c.expand.astype(BF)), 0.0) for v in parts]


def small_rows(masked, c):
    row = jnp.sum(masked, axis=0, keepdims=True)
    return dot((c.expand * row).astype(BF), c.place.astype(BF))


def small_columns(column, c):
    return dot(c.expand.astype(BF), (column.astype(F32) * c.place).astype(BF))


def spread_rows(smalls, c):
    total = None
    for i, v in enumerate(smalls):
        part = dot(c.extra_t(i), v.astype(BF))
        total = part if total is None else total + part
    return total


def column_of(first, index, c):
    wide = dot(c.expand_t.astype(BF), dot(c.extra(index), first).astype(BF))
    return jnp.sum(wide * c.place, axis=1, keepdims=True)


def with_small(rows, smalls, c):
    first = (rows[:, :LANE] + spread_rows(smalls, c)).astype(BF)
    return first, rows[:, LANE:].astype(BF)


def cost(flops, arrays):
    size = sum(int(np.prod(a.shape)) * jnp.dtype(a.dtype).itemsize for a in arrays)
    return pl.CostEstimate(flops=flops, bytes_accessed=size, transcendentals=0)


def call(kernel, name, outs, args, flops, at=None, scratch=(), grant=24):
    out_shape = [jax.ShapeDtypeStruct(s, d) for s, d in outs]
    scalars = [] if at is None else [at]
    return pl.pallas_call(
        kernel,
        out_shape=out_shape,
        in_specs=[pl.BlockSpec(memory_space=pltpu.SMEM)] * len(scalars)
        + [pl.BlockSpec(memory_space=pltpu.VMEM)] * len(args),
        out_specs=[pl.BlockSpec(memory_space=pltpu.VMEM)] * len(outs),
        scratch_shapes=list(scratch),
        name=name,
        cost_estimate=cost(flops, list(args) + out_shape),
        compiler_params=pltpu.CompilerParams(vmem_limit_bytes=grant << 20),
    )(*scalars, *args)


PART = 16
STEP = PART * SLOT


def each_part(body):
    @pl.loop(0, EXP // PART)
    def _(i):
        body(pl.ds(pl.multiple_of(i * STEP, STEP), STEP))


def start_kernel(at, inputs, cotangent, picks0, picks1, gain_own, gain_other, router_own, router_other, *outs):
    send, weights, tokens, grad, gains, routers = outs
    mine = at[0] == 0
    rows = pl.ds(pl.multiple_of(at[0] * TOK, TOK), TOK)
    own, other = gain_own[...], gain_other[...]
    gain0 = jnp.where(mine, own, other)
    gains[0:1, :] = gain0
    gains[1:2, :] = jnp.where(mine, other, own)
    own, other = router_own[...], router_other[...]
    router0 = jnp.where(mine, own, other)
    routers[0] = router0
    routers[1] = jnp.where(mine, other, own)
    token, cot = inputs[rows, :], cotangent[rows, :]
    tokens[...] = token
    grad[...] = cot
    c = Tables(EXP, 2 * SLOT)
    mask, table0 = slots_of(picks0[...], c)
    table1 = slots_of(picks1[...], c, 1.0 * SLOT)[1]
    normed, scale, values = norm(token, gain0)
    weights[...] = mix(normed, router0, mask)
    both = jnp.concatenate([one(table0), one(table1)], axis=0)
    send[...] = dot_t0(both, jnp.concatenate([normed, cot], axis=0)).astype(BF)


def halves_of(x, first, out):
    @pl.loop(0, EXP)
    def _(e):
        source = pl.multiple_of(e * 2 * SLOT + first, 8)
        out[pl.ds(pl.multiple_of(e * SLOT, 8), SLOT), :] = x[pl.ds(source, SLOT), :]


def forward0_kernel(x, wg, wu, wd, out, rows_out, fa, fb, hid):
    halves_of(x, 0, rows_out)

    def part(at):
        gate = dot(rows_out[at, :], wg[...])
        up = dot(rows_out[at, :], wu[...])
        sig = jax.nn.sigmoid(gate)
        act = gate * sig
        hidden = (act * up).astype(BF)
        hid[at, :] = hidden
        fb[at, :] = act
        fa[at, :] = up * sig * (1.0 + gate * (1.0 - sig))
        out[at, :] = dot(hidden, wd[...]).astype(BF)

    each_part(part)


def cotangent_kernel(x, out):
    halves_of(x, SLOT, out)


def expert1_kernel(x, g, wg, wu, wd, send, scaled_out, gate_out, up_out, hid):
    def part(at):
        c = Tables(PART)
        first = x[at, :LANE]
        weight = column_of(first, 0, c) + column_of(first, 1, c)
        gate = dot(x[at, :], wg[...])
        up = dot(x[at, :], wu[...])
        sig = jax.nn.sigmoid(gate)
        act = gate * sig
        hidden = (act * up).astype(BF)
        hid[at, :] = hidden
        out = dot(hidden, wd[...]).astype(BF)
        grad = g[at, :].astype(F32)
        weight_grad = jnp.sum(grad * out.astype(F32), axis=1, keepdims=True)
        scaled = (weight * grad).astype(BF)
        scaled_out[at, :] = scaled
        grad_hidden = dot_t1(scaled, wd[...])
        gate_back = (grad_hidden * (up * sig * (1.0 + gate * (1.0 - sig)))).astype(BF)
        up_back = (grad_hidden * act).astype(BF)
        gate_out[at, :] = gate_back
        up_out[at, :] = up_back
        back = dot_t1(gate_back, wg[...]) + dot_t1(up_back, wu[...])
        smalls = [small_columns(v, c) for v in split3(weight_grad)]
        send[at, :LANE], send[at, LANE:] = with_small(back, smalls, c)

    each_part(part)


def backward0_kernel(x, fa, fb, wd, gate_out, up_out):
    def part(at):
        grad_hidden = dot_t1(x[at, :], wd[...])
        gate_out[at, :] = (grad_hidden * fa[at, :]).astype(BF)
        up_out[at, :] = (grad_hidden * fb[at, :]).astype(BF)

    each_part(part)


def blocks_kernel(near, at, gb, ub, x, sc, hid, sent, kept):
    half, quarter = x.shape[1] // 2, x.shape[1] // 4
    group = at[1] if near else 1 - at[1]
    for which, out in ((1 - at[0], sent), (at[0], kept)):
        rows = x[:, pl.ds(pl.multiple_of(group * half + which * quarter, quarter), quarter)]
        out[0:quarter, :] = dot_t0(rows, gb[...]).astype(BF)
        out[quarter : 2 * quarter, :] = dot_t0(rows, ub[...]).astype(BF)
        low = hid[:, pl.ds(pl.multiple_of(which * quarter, quarter), quarter)]
        wide = sc[:, pl.ds(pl.multiple_of(group * half, half), half)]
        out[2 * quarter :, :] = dot_t0(low, wide).astype(BF)


def rest_kernel(at, x0, x1, x2, gb, ub, wg, wu, layer_gains, gains, out, total):
    total[...] = jnp.zeros_like(total)

    def part(at):
        c = Tables(PART)
        first = x2[at, :LANE]
        back = (dot_t1(gb[at, :], wg[...]) + dot_t1(ub[at, :], wu[...])).astype(BF).astype(F32)
        rows0 = x0[at, :].astype(F32)
        total[0:1, :] += jnp.sum(rows0 * column_of(first, 0, c), axis=0, keepdims=True)
        total[1:2, :] += jnp.sum(rows0 * back, axis=0, keepdims=True)
        total[2:3, :] += jnp.sum(x1[at, :].astype(F32) * column_of(first, 1, c), axis=0, keepdims=True)

    each_part(part)
    gain0 = total[1:2, :] / layer_gains[0:1, :] + gains[1:2, :]
    gain1 = gains[0:1, :]
    mine = at[0] == 0
    column0, column1 = total[0:1, :], total[2:3, :]
    out[0:1, :] = jnp.where(mine, column0, column1)
    out[1:2, :] = jnp.where(mine, gain0, gain1)
    out[2:3, :] = jnp.where(mine, column1, column0)
    out[3:4, :] = jnp.where(mine, gain1, gain0)


def finish_kernel(at, sum0, high0, low1, sum1, *outs):
    quarter = sum0.shape[0] // 3
    mine = at[0] == 0
    for i, out in enumerate(outs):
        rows = slice(i * quarter, (i + 1) * quarter)
        out[0:quarter, :] = jnp.where(mine, sum0[rows, :], low1[rows, :])
        out[quarter:, :] = jnp.where(mine, high0[rows, :], sum1[rows, :])


def middle_kernel(tokens, picks0, weights0, returned, picks1, gains, routers, mixed_out, send, weights1):
    c = Tables(EXP)
    mask0, table0 = slots_of(picks0[...], c)
    hi, lo = weighted(table0, split2(weights0[...]), c)
    back = returned[...]
    mixed = tokens[...].astype(F32) + dot(hi.astype(BF), back) + dot(lo.astype(BF), back)
    mixed = mixed.astype(BF)
    mixed_out[...] = mixed
    mask1, table1 = slots_of(picks1[...], c)
    normed, scale, values = norm(mixed, gains[1:2, :])
    weights = mix(normed, routers[1], mask1)
    weights1[...] = weights
    rows = dot_t0(one(table1), normed)
    smalls = [small_rows(v, c) for v in weighted(table1, split2(weights), c)]
    send[:, :LANE], send[:, LANE:] = with_small(rows, smalls, c)


def turn_kernel(tokens1, picks1, weights1, returned1, grad, tokens0, picks0, weights0, returned0, gains, routers, *outs):
    send, gains_out = outs
    c = Tables(EXP)
    gain0, gain1 = gains[0:1, :], gains[1:2, :]
    mask1, table1 = slots_of(picks1[...], c)
    back1 = returned1[...]
    pick1 = one(table1)
    expert_part = dot(pick1, back1)
    w1 = weights1[...]
    wg1 = jnp.zeros((TOK, EXP), F32)
    for i in range(3):
        column = column_of(back1[:, :LANE], i, c)
        wg1 = wg1 + dot(pick1, (column * c.expand_t).astype(BF))
    lg1 = (w1 * (wg1 - jnp.sum(w1 * wg1, axis=-1, keepdims=True))).astype(BF)
    normed1, scale1, values1 = norm(tokens1[...], gain1)
    normed_grad1 = dot(lg1, routers[1]) + expert_part
    gains_out[0:1, :] = jnp.sum(normed_grad1 * values1 * scale1, axis=0, keepdims=True)
    q = normed_grad1 * gain1
    grad_f = grad[...].astype(F32)
    g0 = (
        grad_f + scale1 * q - scale1 * scale1 * scale1 * values1 * jnp.mean(q * values1, axis=-1, keepdims=True)
    ).astype(BF)
    mask0, table0 = slots_of(picks0[...], c)
    w0 = weights0[...]
    met = jnp.where(table0, dot_t1(g0, returned0[...]), 0.0)
    wg0 = jnp.zeros((TOK, EXP), F32)
    for part in split3(met):
        wg0 = wg0 + dot(part, c.expand_t.astype(BF))
    lg0 = (w0 * (wg0 - jnp.sum(w0 * wg0, axis=-1, keepdims=True))).astype(BF)
    normed0, scale0, values0 = norm(tokens0[...], gain0)
    gains_out[1:2, :] = jnp.sum(dot(lg0, routers[0]) * values0 * scale0, axis=0, keepdims=True)
    hi, lo = weighted(table0, split2(w0), c)
    rows = dot_t0(hi.astype(BF), g0) + dot_t0(lo.astype(BF), g0)
    smalls = [small_rows(weighted(table0, [lg0], c)[0], c), small_rows(weighted(table1, [lg1], c)[0], c)]
    send[:, :LANE], send[:, LANE:] = with_small(rows, smalls, c)


def exchanged(rows):
    return lax.all_to_all(rows, "expert", split_axis=0, concat_axis=0, tiled=True)


def swapped(value):
    return lax.ppermute(value, "pipe", [(0, 1), (1, 0)])


def shards(inputs, cotangent, norm_gain, w_router, w_gate, w_up, w_down, routes):
    pipe = lax.axis_index("pipe")
    data = lax.axis_index("dp")
    at = jnp.stack([pipe, data]).astype(jnp.int32)
    width = inputs.shape[-1]
    inner = w_gate.shape[-1]
    half, quarter = width // 2, width // 4
    first = pipe == 0
    flops = ALL * width * inner

    def part_of(v, which):
        return lax.dynamic_slice_in_dim(v, which * HALF, HALF, 0).reshape(TOK, -1)

    def both(own, other):
        return jnp.where(first, own, other), jnp.where(first, other, own)

    picks0, picks1 = both(part_of(routes[0], pipe), swapped(part_of(routes[0], 1 - pipe)))
    router = w_router[0].T
    rows_shape = ((ALL, width), BF)
    inner_shape = ((ALL, inner), BF)
    few = ((TOK, width), BF)
    send0, weights0, tokens0, grad1, gains, routers = call(
        start_kernel,
        "start",
        [((2 * ALL, width), BF), ((TOK, EXP), F32), few, few, ((2, width), F32), ((2, EXP, width), BF)],
        [
            inputs.reshape(-1, width),
            cotangent.reshape(-1, width),
            picks0,
            picks1,
            norm_gain,
            swapped(norm_gain),
            router,
            swapped(router),
        ],
        400_000_000,
        at,
    )
    arrived = exchanged(send0)
    mats = [both(w[0, 0], swapped(w[0, 0])) for w in (w_gate, w_up, w_down)]
    (gate0, gate1), (up0, up1), (down0, down1) = lax.optimization_barrier(mats)

    out0, recv0, fa0, fb0, hidden0 = call(
        forward0_kernel,
        "forward0",
        [rows_shape, rows_shape, ((ALL, inner), F32), ((ALL, inner), F32), inner_shape],
        [arrived, gate0, up0, down0],
        6 * flops,
    )
    returned0 = exchanged(out0)
    (grad_rows,) = call(cotangent_kernel, "cotangent", [rows_shape], [arrived], 1000)

    tokens1, send1, weights1 = call(
        middle_kernel,
        "middle",
        [few, rows_shape, ((TOK, EXP), F32)],
        [tokens0, picks0, weights0, returned0, picks1, gains, routers],
        600_000_000,
    )
    recv1 = exchanged(send1)
    send_b, scaled1, gate_back1, up_back1, hidden1 = call(
        expert1_kernel,
        "expert1",
        [rows_shape, rows_shape, inner_shape, inner_shape, inner_shape],
        [recv1, grad_rows, gate1, up1, down1],
        12 * flops,
    )
    returned1 = exchanged(send_b)

    block = ((3 * quarter, half), BF)

    def blocks(near, args, name):
        return call(functools.partial(blocks_kernel, near), name, [block, block], args, 3 * flops, at)

    def far_part(args, name):
        sent, kept = blocks(False, args, name)
        paired = (kept.astype(F32) + swapped(sent).astype(F32)).astype(BF)
        return lax.ppermute(paired, "dp", [(0, 1), (1, 0)])

    def near_part(got, args, name):
        sent, kept = blocks(True, args, name)
        return (kept.astype(F32) + swapped(sent).astype(F32) + got.astype(F32)).astype(BF)

    args1 = [gate_back1, up_back1, recv1, scaled1, hidden1]
    sum1 = near_part(far_part(args1, "far1"), args1, "near1")
    low1 = lax.ppermute(sum1, "pipe", [(0, 1)])

    send2, token_gains = call(
        turn_kernel,
        "turn",
        [rows_shape, ((2, width), F32)],
        [tokens1, picks1, weights1, returned1, grad1, tokens0, picks0, weights0, returned0, gains, routers],
        900_000_000,
    )
    recv2 = exchanged(send2)
    gate_back0, up_back0 = call(
        backward0_kernel, "backward0", [inner_shape, inner_shape], [recv2, fa0, fb0, down0], 2 * flops
    )
    args0 = [gate_back0, up_back0, recv0, recv2, hidden0]
    got0 = far_part(args0, "far0")
    (small,) = call(
        rest_kernel,
        "rest",
        [((4, width), F32)],
        [recv0, recv1, recv2, gate_back0, up_back0, gate0, up0, gains, token_gains],
        4 * flops,
        at,
        [pltpu.VMEM((8, width), F32)],
    )
    mine = small[0:2] + swapped(small[2:4])
    group = 2 * EXP
    told = jnp.broadcast_to(mine.reshape(1, 2 * width // LANE, LANE), (group, 2 * width // LANE, LANE))
    heard = lax.all_to_all(told, ("dp", "expert"), split_axis=0, concat_axis=0, tiled=True)
    heard = heard.reshape(2, EXP, 2, width)
    router_sum = (heard[0, :, 0] + heard[1, :, 0]).T
    gain_sum = jnp.sum(heard[:, :, 1], axis=(0, 1))

    small, hidden0 = lax.optimization_barrier((small, hidden0))
    sum0 = near_part(got0, args0[:4] + [hidden0], "near0")
    high0 = lax.ppermute(sum0, "pipe", [(1, 0)])
    final = ((2 * quarter, half), BF)
    outs = call(finish_kernel, "finish", [final] * 3, [sum0, high0, low1, sum1], 1000, at)
    return (
        outs[0][None, None],
        outs[1][None, None],
        outs[2][None, None],
        router_sum[None],
        gain_sum[None],
    )


def solution(mesh):
    in_specs = (
        P(None, ("dp", "expert"), None),
        P(None, ("dp", "expert"), None),
        P("pipe", None),
        P("pipe", None, None),
        P("pipe", "expert", None, None),
        P("pipe", "expert", None, None),
        P("pipe", "expert", None, None),
        P("pipe", None, ("dp", "expert"), None),
    )
    out_specs = (
        P("pipe", "expert", "dp", None),
        P("pipe", "expert", "dp", None),
        P("pipe", "expert", None, "dp"),
        P("pipe", None, None),
        P("pipe", None),
    )
    return jax.shard_map(shards, mesh=mesh, in_specs=in_specs, out_specs=out_specs, check_vma=False)
```

```python
import jax
import jax.numpy as jnp
import numpy as np
from jax import lax
from jax.experimental import pallas as pl
from jax.experimental.pallas import tpu as pltpu
from jax.sharding import PartitionSpec as P


EPS = 1e-05
BF = jnp.bfloat16
F32 = jnp.float32

ROWS = 32
CAP = 10
HALF = 2
TOK = ROWS * HALF
EXP = 32
USED = CAP * HALF
LANE = 128
LINES = 8
PACK = EXP * LINES
REST = USED - 2 * LINES
ALL = EXP * USED
PARTS = ((0, PACK), (PACK, ALL - PACK))


def dot(a, b):
    return lax.dot_general(a, b, (((1,), (0,)), ((), ())), preferred_element_type=F32)


def dot_t0(a, b):
    return lax.dot_general(a, b, (((0,), (0,)), ((), ())), preferred_element_type=F32)


def dot_t1(a, b):
    return lax.dot_general(a, b, (((1,), (1,)), ((), ())), preferred_element_type=F32)


def split2(v):
    hi = v.astype(BF)
    return hi, (v - hi.astype(F32)).astype(BF)


def split3(v):
    hi = v.astype(BF)
    rest = v - hi.astype(F32)
    mid = rest.astype(BF)
    return hi, mid, (rest - mid.astype(F32)).astype(BF)


def flags(test):
    return jnp.where(test, 1.0, 0.0).astype(BF)


def count(shape, axis):
    return lax.broadcasted_iota(jnp.int32, shape, axis).astype(F32)


def over(v, by):
    whole = jnp.floor((v + 0.5) * (1.0 / by))
    return whole, v - by * whole


def row_place(first, shape, axis):
    s = count(shape, axis) + first
    group, inner = over(s, PACK)
    source, line = over(inner, LINES)
    source_rest, line_rest = over(inner, REST)
    rest = group >= 2
    return jnp.where(rest, source_rest, source), jnp.where(rest, line_rest, line) + LINES * group


def line_place(shape, axis):
    return over(count(shape, axis), LINES)


def column_place(shape, axis):
    group, inner = over(count(shape, axis), PACK)
    partner, line = over(inner, LINES)
    slot = jnp.where(group >= 3, jnp.where(line >= REST, line + (2 * LINES - REST), -9.0), line + LINES * group)
    return partner, slot


def expand_of():
    shape = (EXP, 4 * PACK)
    return flags(column_place(shape, 1)[0] == count(shape, 0))


def expand_t_of():
    shape = (4 * PACK, EXP)
    return flags(column_place(shape, 0)[0] == count(shape, 1))


def slots_of(picks, expand):
    columns = lax.broadcasted_iota(jnp.int32, (TOK, EXP), 1)
    mask = jnp.zeros((TOK, EXP), F32)
    for k in range(picks.shape[1]):
        mask = mask + jnp.where(picks[:, k : k + 1] == columns, 1.0, 0.0)
    row = lax.broadcasted_iota(jnp.int32, (TOK, TOK), 0)
    column = lax.broadcasted_iota(jnp.int32, (TOK, TOK), 1)
    earlier = flags((column < row) & ((row < ROWS) | (column >= ROWS)))
    start = jnp.where(lax.broadcasted_iota(jnp.int32, (TOK, EXP), 0) < ROWS, 0.0, 1.0 * CAP)
    slot = mask * (dot(earlier, mask.astype(BF)) + start + 1.0) - 1.0
    table = dot(slot.astype(BF), expand) == column_place((1, 4 * PACK), 1)[1]
    return mask, table, slot


def norm(tokens, gain):
    values = tokens.astype(F32)
    scale = lax.rsqrt(jnp.mean(values * values, axis=-1, keepdims=True) + EPS)
    return (values * scale * gain).astype(BF), scale, values


def mix(normed, router, mask):
    logits = dot_t1(normed, router)
    expo = jnp.where(mask > 0.0, jnp.exp(jnp.where(mask > 0.0, logits, 0.0)), 0.0)
    return expo / jnp.sum(expo, axis=-1, keepdims=True)


def weighted(table, parts, expand):
    return [jnp.where(table, dot(v, expand), 0.0).astype(BF) for v in parts]


def to_packed(picked, rows, out, done, first=0):
    half = rows.shape[1] // 2
    width = 2 * half
    for i in range(2):
        columns = slice(i * PACK, (i + 1) * PACK)
        out[:, first + i * width : first + (i + 1) * width] = sum(dot_t0(v[:, columns], rows) for v in picked).astype(BF)
        done(i)
    low, high = slice(2 * PACK, 3 * PACK), slice(3 * PACK, 4 * PACK)
    last = sum(dot_t0(v[:, low], rows[:, :half]) + dot_t0(v[:, high], rows[:, half:]) for v in picked)
    out[:, first + 2 * width : first + 2 * width + half] = last.astype(BF)
    done(2)


def from_packed(picked, packed, width):
    half = width // 2
    rest = packed[:, 2 * width : 2 * width + half]
    total = sum(
        dot(v[:, :PACK], packed[:, :width]) + dot(v[:, PACK : 2 * PACK], packed[:, width : 2 * width]) for v in picked
    )
    low = sum(dot(v[:, 2 * PACK : 3 * PACK], rest) for v in picked)
    high = sum(dot(v[:, 3 * PACK :], rest) for v in picked)
    return total + jnp.concatenate([low, high], axis=1)


def rest_tables():
    shape = (EXP * REST, PACK)
    source, line = over(count(shape, 0), REST)
    place, at = line_place(shape, 1)
    return flags((source == place) & (line == at)), flags((source == place) & (line + REST == at))


def unpack(packed, first, width, out, piece):
    if piece == 0:
        out[0:PACK, :] = packed[:, first : first + width]
        return
    half = width // 2
    out[PACK : 2 * PACK, :] = packed[:, first + width : first + 2 * width]
    rest = packed[:, first + 2 * width : first + 2 * width + half]
    low, high = rest_tables()
    out[2 * PACK :, :half] = dot(low, rest).astype(BF)
    out[2 * PACK :, half:] = dot(high, rest).astype(BF)


def pack(rows, out, piece):
    width = rows.shape[1]
    if piece == 0:
        out[:, :width] = rows
        return
    half = width // 2
    out[:, width : 2 * width] = rows[:PACK, :]
    low, high = rest_tables()
    rest = dot_t0(low, rows[PACK:, :half]) + dot_t0(high, rows[PACK:, half:])
    out[:, 2 * width : 2 * width + half] = rest.astype(BF)


def line_table(first, number, test):
    shape = (number, PACK)
    source, line = line_place(shape, 1)
    return flags((row_place(first, shape, 0)[0] == source) & test(line))


def slot_lanes(first, number):
    shape = (number, LANE)
    return row_place(first, shape, 0)[1] == count(shape, 1)


def column_of(small, first, number, test):
    wide = dot(line_table(first, number, test), small)
    return jnp.sum(jnp.where(slot_lanes(first, number), wide, 0.0), axis=1, keepdims=True)


def small_lines(masked):
    shape = (3 * PACK, LANE)
    place = flags(column_place(shape, 0)[1] == count(shape, 1))
    shape = (PACK, 3 * PACK)
    source, line = line_place(shape, 0)
    same = source == column_place(shape, 1)[0]
    total = None
    for i, v in enumerate(masked):
        row = jnp.sum(v[:, : 3 * PACK].astype(F32), axis=0, keepdims=True)
        part = dot(jnp.where(same & (line == i), row, 0.0).astype(BF), place)
        total = part if total is None else total + part
    return total.astype(BF)


def cost(flops, arrays):
    size = sum(int(np.prod(a.shape)) * jnp.dtype(a.dtype).itemsize for a in arrays)
    return pl.CostEstimate(flops=flops, bytes_accessed=size, transcendentals=0)


def cuts(sizes):
    return [(sum(sizes[:i]), size) for i, size in enumerate(sizes)]


def view(ref, axis, cut):
    return ref.at[(slice(None),) * axis + (pl.ds(*cut),)]


class Load:
    def __init__(self, array, sizes=None, axis=0, first=0, width=None):
        self.array, self.axis, self.first = array, axis, first
        self.width = width or array.shape[-1]
        self.shape = tuple(array.shape[:-1]) + (self.width,)
        self.dtype = array.dtype
        self.cuts = cuts(sizes or (self.shape[axis],))
        self.other = None

    def copies(self, src, dst, sem, at):
        if self.width != self.array.shape[-1]:
            src = view(src, len(self.shape) - 1, (self.first, self.width))
        return [
            pltpu.make_async_copy(view(src, self.axis, cut), view(dst, self.axis, cut), sem.at[i])
            for i, cut in enumerate(self.cuts)
        ]


class Tokens(Load):
    def __init__(self, array):
        super().__init__(array)
        self.shape = (TOK, array.shape[1])
        self.cuts = [(0, TOK)]

    def copies(self, src, dst, sem, at):
        return [pltpu.make_async_copy(src.at[pl.ds(pl.multiple_of(at[0] * TOK, TOK), TOK)], dst, sem.at[0])]


class Either(Load):
    def __init__(self, array, other, sizes):
        super().__init__(array, sizes)
        self.other = other


class Moves:
    def __init__(self, loads, stores):
        self.loads, self.stores, self.taken = loads, stores, set()

    def start(self, order):
        for i, piece in order or [(i, p) for i, load in enumerate(self.loads) for p in range(len(load))]:
            self.loads[i][piece].start()

    def need(self, *names):
        for name in names:
            i, piece = name if isinstance(name, tuple) else (name, None)
            for p in range(len(self.loads[i])) if piece is None else [piece]:
                if (i, p) not in self.taken:
                    self.taken.add((i, p))
                    self.loads[i][p].wait()

    def flush(self, piece, *outs):
        for j in outs:
            self.stores[j][piece].start()

    def end(self):
        self.need(*range(len(self.loads)))
        for store in self.stores:
            for copy in store:
                copy.wait()


def call(body, outs, args, flops, at=None, scratch=(), order=None):
    args = [v if isinstance(v, Load) else Load(v) for v in args]
    others = [v.other for v in args if v.other is not None]
    out_shape = [jax.ShapeDtypeStruct(out[0], out[1]) for out in outs]
    ways = [(out[2], cuts(out[3])) if len(out) > 2 else (0, [(0, out[0][0])]) for out in outs]
    scalars = [] if at is None else [at]
    n, m = len(args), len(outs)

    def kernel(*refs):
        where = refs[0] if scalars else None
        refs = refs[len(scalars) :]
        ins, twins, refs = refs[:n], refs[n : n + len(others)], refs[n + len(others) :]
        results, held, refs = refs[:m], refs[m : m + n], refs[m + n :]
        made, load_sems, store_sems = refs[:m], refs[m : m + n], refs[m + n : m + n + m]
        own = refs[m + n + m :]
        loads = [v.copies(src, dst, sem, where) for v, src, dst, sem in zip(args, ins, held, load_sems)]
        stores = [
            [
                pltpu.make_async_copy(view(made[j], axis, cut), view(results[j], axis, cut), store_sems[j].at[i])
                for i, cut in enumerate(pieces)
            ]
            for j, (axis, pieces) in enumerate(ways)
        ]
        moves = Moves(loads, stores)
        if others:
            for pick, sources in enumerate((ins, twins)):

                @pl.when(where[0] == pick)
                def _():
                    picked = [v.copies(*way, where) for v, *way in zip(args, sources, held, load_sems)]
                    for piece in range(len(args[0].cuts)):
                        for copies in picked:
                            copies[piece].start()

        else:
            moves.start(order)
        body(moves, where, held, made, *own)
        moves.end()

    hbm = pl.BlockSpec(memory_space=pl.ANY)
    return pl.pallas_call(
        kernel,
        out_shape=out_shape,
        in_specs=[pl.BlockSpec(memory_space=pltpu.SMEM)] * len(scalars) + [hbm] * (n + len(others)),
        out_specs=[hbm] * m,
        scratch_shapes=[pltpu.VMEM(v.shape, v.dtype) for v in args]
        + [pltpu.VMEM(s.shape, s.dtype) for s in out_shape]
        + [pltpu.SemaphoreType.DMA((len(v.cuts),)) for v in args]
        + [pltpu.SemaphoreType.DMA((len(pieces),)) for axis, pieces in ways]
        + list(scratch),
        cost_estimate=cost(flops, [v.array for v in args] + out_shape),
        compiler_params=pltpu.CompilerParams(vmem_limit_bytes=63 << 20),
    )(*scalars, *[v.array for v in args], *others)


def start_body(moves, at, ins, outs):
    inputs, cotangent, picks0, picks1, gain_own, gain_other, router_own, router_other = ins
    send, weights, tokens, grad, gains, routers = outs
    mine = at[0] == 0
    expand = expand_of()
    moves.need(2, 3)
    mask, table0, _ = slots_of(picks0[...], expand)
    table1 = slots_of(picks1[...], expand)[1]
    moves.need(0, 1, 4, 5)
    own, other = gain_own[...], gain_other[...]
    gain0 = jnp.where(mine, own, other)
    gains[0:1, :] = gain0
    gains[1:2, :] = jnp.where(mine, other, own)
    token, cot = inputs[...], cotangent[...]
    normed, _, _ = norm(token, gain0)
    to_packed([flags(table0)], normed, send, lambda i: moves.flush(i, 0))
    to_packed([flags(table1)], cot, send, lambda i: moves.flush(3 + i, 0), send.shape[1] // 2)
    tokens[...] = token
    grad[...] = cot
    moves.need(6, 7)
    own, other = router_own[...], router_other[...]
    router0 = jnp.where(mine, own, other)
    routers[0:EXP, :] = router0
    routers[EXP:, :] = jnp.where(mine, other, own)
    weights[...] = mix(normed, router0, mask)
    moves.flush(0, 1, 2, 3, 4, 5)


def forward_body(moves, at, ins, outs, rows):
    x, wg, wu, wd = ins
    (out,) = outs
    width = rows.shape[1]
    for i, (first, number) in enumerate(PARTS):
        part = pl.ds(first, number)
        moves.need(*[(0, 0)] if i == 0 else [(0, 1), (0, 2)])
        unpack(x, 0, width, rows, i)
        moves.need(1)
        gate = dot(rows[part, :], wg[...])
        moves.need(2)
        up = dot(rows[part, :], wu[...])
        hidden = (jax.nn.silu(gate) * up).astype(BF)
        moves.need(3)
        pack(dot(hidden, wd[...]).astype(BF), out, i)
        for piece in [0] if i == 0 else [1, 2]:
            moves.flush(piece, 0)


def residual_body(moves, at, ins, outs):
    x, wg, wu = ins
    fa, fb, hid, rows, grad = outs
    width = rows.shape[1]
    for i, (first, number) in enumerate(PARTS):
        part = pl.ds(first, number)
        moves.need(0, 1)
        unpack(x, 0, width, rows, i)
        unpack(x, x.shape[1] // 2, width, grad, i)
        gate = dot(rows[part, :], wg[...])
        moves.need(2)
        up = dot(rows[part, :], wu[...])
        sig = jax.nn.sigmoid(gate)
        act = gate * sig
        hid[part, :] = (act * up).astype(BF)
        fb[part, :] = act
        fa[part, :] = up * sig * (1.0 + gate * (1.0 - sig))
        moves.flush(i, 0, 1, 2, 3, 4)


def expert1_body(moves, at, ins, outs):
    x, g, wg, wu, wd = ins
    send, rows, scaled_out, gate_out, up_out, hid = outs
    width = rows.shape[1]
    moves.need(0)
    small = x[:, x.shape[1] - LANE :]
    told = [jnp.zeros((PACK, LANE), F32) for _ in range(3)]
    for i, (first, number) in enumerate(PARTS):
        part = pl.ds(first, number)
        unpack(x, 0, width, rows, i)
        moves.need(2)
        gate = dot(rows[part, :], wg[...])
        moves.need(3)
        up = dot(rows[part, :], wu[...])
        sig = jax.nn.sigmoid(gate)
        act = gate * sig
        hidden = (act * up).astype(BF)
        hid[part, :] = hidden
        moves.need(4)
        out = dot(hidden, wd[...]).astype(BF)
        weight = column_of(small, first, number, lambda line: line < 2)
        moves.need((1, i))
        grad = g[part, :].astype(F32)
        weight_grad = jnp.sum(grad * out.astype(F32), axis=1, keepdims=True)
        scaled = (weight * grad).astype(BF)
        scaled_out[part, :] = scaled
        grad_hidden = dot_t1(scaled, wd[...])
        gate_back = (grad_hidden * (up * sig * (1.0 + gate * (1.0 - sig)))).astype(BF)
        up_back = (grad_hidden * act).astype(BF)
        gate_out[part, :] = gate_back
        up_out[part, :] = up_back
        pack((dot_t1(gate_back, wg[...]) + dot_t1(up_back, wu[...])).astype(BF), send, i)
        placed = jnp.where(slot_lanes(first, number), weight_grad, 0.0)
        for k, v in enumerate(split3(placed)):
            told[k] = told[k] + dot_t0(line_table(first, number, lambda line: line == k), v)
        moves.flush(i, 1, 2, 3, 4, 5)
        if i == 0:
            moves.flush(0, 0)
    send[:, send.shape[1] - LANE :] = (told[0] + told[1] + told[2]).astype(BF)
    moves.flush(1, 0)
    moves.flush(2, 0)


def blocks_of(gb, ub, x, sc, hid, group, which, out):
    half, quarter = x.shape[1] // 2, x.shape[1] // 4
    rows = x[:, pl.ds(pl.multiple_of(group * half + which * quarter, quarter), quarter)]
    gate = dot_t0(rows, gb[...])
    up = dot_t0(rows, ub[...])
    out[0:quarter, :] = gate.astype(BF)
    out[quarter : 2 * quarter, :] = up.astype(BF)
    low = hid[:, pl.ds(pl.multiple_of(which * quarter, quarter), quarter)]
    wide = sc[:, pl.ds(pl.multiple_of(group * half, half), half)]
    out[2 * quarter :, :] = dot_t0(low, wide).astype(BF)
    return gate, up


def four_blocks(at):
    return [(group, which) for group in (1 - at[1], at[1]) for which in (1 - at[0], at[0])]


def grads1_body(moves, at, ins, outs):
    gb, ub, x, sc, hid = ins
    moves.need(0, 1, 2, 3, 4)
    for j, (group, which) in enumerate(four_blocks(at)):
        blocks_of(gb, ub, x, sc, hid, group, which, outs[j])
        moves.flush(0, j)


def backward0_body(moves, at, ins, outs, rows, gb, ub, total):
    sc, fa, fb, wd, x, hid, wg, wu, x1, layer_gains, gains = ins
    mine, theirs = outs[4:]
    width = rows.shape[1]
    moves.need(3)
    for i, (first, number) in enumerate(PARTS):
        part = pl.ds(first, number)
        moves.need(*[(0, 0)] if i == 0 else [(0, 1), (0, 2)])
        moves.need((1, i), (2, i))
        unpack(sc, 0, width, rows, i)
        grad_hidden = dot_t1(rows[part, :], wd[...])
        gb[part, :] = (grad_hidden * fa[part, :]).astype(BF)
        ub[part, :] = (grad_hidden * fb[part, :]).astype(BF)
    moves.need(4, 5, 6, 7)
    half, quarter = width // 2, width // 4
    shape = (quarter, quarter)
    same = lax.broadcasted_iota(jnp.int32, shape, 0) == lax.broadcasted_iota(jnp.int32, shape, 1)
    for j, (group, which) in enumerate(four_blocks(at)):
        gate, up = blocks_of(gb, ub, x, rows, hid, group, which, outs[j])
        moves.flush(0, j)
        place = pl.ds(pl.multiple_of(group * half + which * quarter, quarter), quarter)
        column = jnp.sum(gate * wg[place, :].astype(F32) + up * wu[place, :].astype(F32), axis=1, keepdims=True)
        total[1:2, place] = jnp.sum(jnp.where(same, column, 0.0), axis=0, keepdims=True)
    moves.need(8, 9, 10)
    small = sc[:, sc.shape[1] - LANE :]
    for line, array, index in ((0, x, 0), (2, x1, 1)):
        column = column_of(small, 0, ALL, lambda at_line: at_line == index)
        wide = jnp.broadcast_to(column, (ALL, LANE)).astype(BF)
        total[line : line + 1, :] = dot_t0(wide, array[...])[0:1, :]
    gain0 = total[1:2, :] / layer_gains[0:1, :] + gains[1:2, :]
    gain1 = gains[0:1, :]
    first = at[0] == 0
    column0, column1 = total[0:1, :], total[2:3, :]
    mine[0:1, :] = jnp.where(first, column0, column1)
    mine[1:2, :] = jnp.where(first, gain0, gain1)
    theirs[0:1, :] = jnp.where(first, column1, column0)
    theirs[1:2, :] = jnp.where(first, gain1, gain0)
    moves.flush(0, 4, 5)


def told_body(moves, at, ins, outs):
    own, other = ins
    (out,) = outs
    moves.need(0, 1)
    group, lines, lane = out.shape
    both = own[...] + other[...]
    for v in range(2):
        for j in range(lines // 2):
            piece = both[v : v + 1, j * lane : (j + 1) * lane]
            out[:, v * (lines // 2) + j, :] = jnp.broadcast_to(piece, (group, lane))
    moves.flush(0, 0)


def heard_body(moves, at, ins, outs):
    (heard,) = ins
    router, gain = outs
    moves.need(0)
    _, lines, lane = heard.shape
    for j in range(lines // 2):
        column = slice(j * lane, (j + 1) * lane)
        router[:, column] = heard[0:EXP, j, :] + heard[EXP:, j, :]
        gain[:, column] = jnp.sum(heard[:, lines // 2 + j, :], axis=0, keepdims=True)
    moves.flush(0, 0, 1)


def finish_body(moves, at, ins, outs):
    low, high, low_got, high_got = ins
    quarter = low.shape[0] // 3
    for i, out in enumerate(outs):
        moves.need(*[(k, i) for k in range(4)])
        rows = slice(i * quarter, (i + 1) * quarter)
        out[0:quarter, :] = (low[rows, :].astype(F32) + low_got[rows, :].astype(F32)).astype(BF)
        out[quarter:, :] = (high[rows, :].astype(F32) + high_got[rows, :].astype(F32)).astype(BF)
        moves.flush(0, i)


def middle_body(moves, at, ins, outs):
    tokens, picks0, weights0, returned, picks1, gains, routers = ins
    mixed_out, send, weights1 = outs
    width = tokens.shape[1]
    expand = expand_of()
    moves.need(1, 2, 4)
    _, table0, _ = slots_of(picks0[...], expand)
    parts = weighted(table0, split2(weights0[...]), expand)
    mask1, table1, _ = slots_of(picks1[...], expand)
    moves.need(0, 3, 5, 6)
    mixed = (tokens[...].astype(F32) + from_packed(parts, returned, width)).astype(BF)
    mixed_out[...] = mixed
    normed, _, _ = norm(mixed, gains[1:2, :])
    weights = mix(normed, routers[EXP:, :], mask1)
    weights1[...] = weights
    send[:, send.shape[1] - LANE :] = small_lines(weighted(table1, split2(weights), expand))
    to_packed([flags(table1)], normed, send, lambda i: moves.flush(i, 1))
    moves.flush(0, 0, 2)


def turn_body(moves, at, ins, outs):
    tokens1, picks1, weights1, returned1, grad, tokens0, picks0, weights0, returned0, gains, routers = ins
    send, gains_out = outs
    width = tokens1.shape[1]
    half = width // 2
    expand = expand_of()
    moves.need(0, 1, 2, 4, 5, 6, 7, 9, 10)
    gain0, gain1 = gains[0:1, :], gains[1:2, :]
    _, table1, slot1 = slots_of(picks1[...], expand)
    _, table0, _ = slots_of(picks0[...], expand)
    w0, w1 = weights0[...], weights1[...]
    parts0 = weighted(table0, split2(w0), expand)
    _, scale0, values0 = norm(tokens0[...], gain0)
    _, scale1, values1 = norm(tokens1[...], gain1)
    moves.need(3)
    expert_part = from_packed([flags(table1)], returned1, width)
    shape = (PACK, EXP)
    source, line = line_place(shape, 0)
    told = dot_t0(returned1[:, returned1.shape[1] - LANE :], flags((source == count(shape, 1)) & (line < 3)))
    wg1 = jnp.zeros((TOK, EXP), F32)
    for i in range(USED):
        wg1 = jnp.where(slot1 == i, told[i : i + 1, :], wg1)
    lg1 = (w1 * (wg1 - jnp.sum(w1 * wg1, axis=-1, keepdims=True))).astype(BF)
    normed_grad1 = dot(lg1, routers[EXP:, :]) + expert_part
    gains_out[0:1, :] = jnp.sum(normed_grad1 * values1 * scale1, axis=0, keepdims=True)
    q = normed_grad1 * gain1
    grad_f = grad[...].astype(F32)
    g0 = (
        grad_f + scale1 * q - scale1 * scale1 * scale1 * values1 * jnp.mean(q * values1, axis=-1, keepdims=True)
    ).astype(BF)
    moves.need(8)
    rest = returned0[:, 2 * width : 2 * width + half]
    met = jnp.concatenate(
        [
            dot_t1(g0, returned0[:, :width]),
            dot_t1(g0, returned0[:, width : 2 * width]),
            dot_t1(g0[:, :half], rest),
            dot_t1(g0[:, half:], rest),
        ],
        axis=1,
    )
    met = jnp.where(table0, met, 0.0)
    expand_t = expand_t_of()
    wg0 = jnp.zeros((TOK, EXP), F32)
    for part in split3(met):
        wg0 = wg0 + dot(part, expand_t)
    lg0 = (w0 * (wg0 - jnp.sum(w0 * wg0, axis=-1, keepdims=True))).astype(BF)
    gains_out[1:2, :] = jnp.sum(dot(lg0, routers[0:EXP, :]) * values0 * scale0, axis=0, keepdims=True)
    lines = [weighted(table0, [lg0], expand)[0], weighted(table1, [lg1], expand)[0]]
    send[:, send.shape[1] - LANE :] = small_lines(lines)
    to_packed(parts0, g0, send, lambda i: moves.flush(i, 0))
    moves.flush(0, 1)


def exchanged(rows):
    return lax.all_to_all(rows, "expert", split_axis=0, concat_axis=0, tiled=True)


def swapped(value):
    return lax.ppermute(value, "pipe", [(0, 1), (1, 0)])


def shards(inputs, cotangent, norm_gain, w_router, w_gate, w_up, w_down, routes):
    pipe = lax.axis_index("pipe")
    data = lax.axis_index("dp")
    at = jnp.stack([pipe, data]).astype(jnp.int32)
    width = inputs.shape[-1]
    inner = w_gate.shape[-1]
    half, quarter = width // 2, width // 4
    first = pipe == 0
    flops = ALL * width * inner

    def part_of(v, which):
        return lax.dynamic_slice_in_dim(v, which * HALF, HALF, 0).reshape(TOK, -1)

    def both(own, other):
        return jnp.where(first, own, other), jnp.where(first, other, own)

    picks0, picks1 = both(part_of(routes[0], pipe), swapped(part_of(routes[0], 1 - pipe)))
    router = w_router[0].T
    packed = 2 * width + half
    pieces = (width, width, half)
    with_small = (width, width, half + LANE)
    part_rows = [number for first, number in PARTS]
    rows_shape = ((ALL, width), BF, 0, part_rows)
    inner_shape = ((ALL, inner), BF, 0, part_rows)
    wide_shape = ((ALL, inner), F32, 0, part_rows)
    small_shape = ((PACK, packed + LANE), BF, 1, with_small)
    few = ((TOK, width), BF)
    send0, weights0, tokens0, grad1, gains, routers = call(
        start_body,
        [((PACK, 2 * packed), BF, 1, pieces * 2), ((TOK, EXP), F32), few, few, ((2, width), F32), ((2 * EXP, width), BF)],
        [
            Tokens(inputs.reshape(-1, width)),
            Tokens(cotangent.reshape(-1, width)),
            picks0,
            picks1,
            norm_gain,
            swapped(norm_gain),
            router,
            swapped(router),
        ],
        400_000_000,
        at,
    )
    arrived = exchanged(send0)
    mats = [both(w[0, 0], swapped(w[0, 0])) for w in (w_gate, w_up, w_down)]
    (gate0, gate1), (up0, up1), (down0, down1) = lax.optimization_barrier(mats)

    (out0,) = call(
        forward_body,
        [((PACK, packed), BF, 1, pieces)],
        [Load(arrived, pieces, 1, 0, packed), gate0, up0, down0],
        6 * flops,
        scratch=[pltpu.VMEM((ALL, width), BF)],
        order=[(0, 0), (1, 0), (2, 0), (3, 0), (0, 1), (0, 2)],
    )
    returned0 = exchanged(out0)
    fa0, fb0, hidden0, recv0, grad_rows = call(
        residual_body, [wide_shape, wide_shape, inner_shape, rows_shape, rows_shape], [arrived, gate0, up0], 4 * flops
    )
    returned0, grad_rows = lax.optimization_barrier((returned0, grad_rows))

    tokens1, send1, weights1 = call(
        middle_body,
        [few, small_shape, ((TOK, EXP), F32)],
        [tokens0, picks0, weights0, returned0, picks1, gains, routers],
        600_000_000,
    )
    arrived1 = exchanged(send1)
    send_b, rows1, scaled1, gate_back1, up_back1, hidden1 = call(
        expert1_body,
        [small_shape, rows_shape, rows_shape, inner_shape, inner_shape, inner_shape],
        [arrived1, Load(grad_rows, part_rows), gate1, up1, down1],
        12 * flops,
        order=[(0, 0), (2, 0), (3, 0), (4, 0), (1, 0), (1, 1)],
    )
    returned1 = exchanged(send_b)

    block = ((3 * quarter, half), BF)

    def to_owner(paired, owner):
        return [
            lax.ppermute(paired, ("dp", "pipe"), [(2 * d + p, 2 * (1 - d) + owner) for d in range(2)]) for p in range(2)
        ]

    def paired_of(kept, swap):
        return (kept.astype(F32) + swap.astype(F32)).astype(BF)

    args1 = [gate_back1, up_back1, rows1, scaled1, hidden1]
    sent, kept, sent_near, kept_near = call(grads1_body, [block] * 4, args1, 6 * flops, at)
    paired1 = paired_of(kept, swapped(sent))
    got1 = to_owner(paired1, 1)

    send2, token_gains = call(
        turn_body,
        [small_shape, ((2, width), F32)],
        [tokens1, picks1, weights1, returned1, grad1, tokens0, picks0, weights0, returned0, gains, routers],
        900_000_000,
    )
    recv2 = exchanged(send2)
    sum1 = paired_of(kept_near, swapped(sent_near))
    low1 = lax.ppermute(sum1, "pipe", [(0, 1)])
    recv2, low1, sum1, got1 = lax.optimization_barrier((recv2, low1, sum1, got1))

    few_rows = ((2, width), F32)
    sent, kept, sent_near, kept_near, small, others = call(
        backward0_body,
        [block] * 4 + [few_rows] * 2,
        [Load(recv2, with_small, 1), Load(fa0, part_rows), Load(fb0, part_rows), down0, recv0, hidden0]
        + [gate0, up0, rows1, gains, token_gains],
        9 * flops,
        at,
        [pltpu.VMEM((ALL, width), BF), pltpu.VMEM((ALL, inner), BF), pltpu.VMEM((ALL, inner), BF)]
        + [pltpu.VMEM((8, width), F32)],
        order=[(3, 0), (0, 0), (1, 0), (2, 0), (0, 1), (0, 2), (1, 1), (2, 1)] + [(i, 0) for i in range(4, 11)],
    )
    paired0 = paired_of(kept, swapped(sent))
    got0 = to_owner(paired0, 0)
    told = call(told_body, [((2 * EXP, 2 * width // LANE, LANE), F32)], [small, swapped(others)], 1000)[0]
    heard = lax.all_to_all(told, ("dp", "expert"), split_axis=0, concat_axis=0, tiled=True)
    sum0 = paired_of(kept_near, swapped(sent_near))
    high0 = lax.ppermute(sum0, "pipe", [(1, 0)])
    router_sum, gain_sum = call(heard_body, [((EXP, width), F32), ((1, width), F32)], [heard], 1000)
    thirds = (quarter,) * 3
    final = ((2 * quarter, half), BF)
    outs = call(
        finish_body,
        [final] * 3,
        [
            Either(sum0, low1, thirds),
            Either(high0, sum1, thirds),
            Either(got0[0], got1[0], thirds),
            Either(got0[1], got1[1], thirds),
        ],
        1000,
        at,
    )
    return (
        outs[0][None, None],
        outs[1][None, None],
        outs[2][None, None],
        router_sum.T[None],
        gain_sum,
    )


def solution(mesh):
    in_specs = (
        P(None, ("dp", "expert"), None),
        P(None, ("dp", "expert"), None),
        P("pipe", None),
        P("pipe", None, None),
        P("pipe", "expert", None, None),
        P("pipe", "expert", None, None),
        P("pipe", "expert", None, None),
        P("pipe", None, ("dp", "expert"), None),
    )
    out_specs = (
        P("pipe", "expert", "dp", None),
        P("pipe", "expert", "dp", None),
        P("pipe", "expert", None, "dp"),
        P("pipe", None, None),
        P("pipe", None),
    )

    return jax.shard_map(shards, mesh=mesh, in_specs=in_specs, out_specs=out_specs, check_vma=False)
```

```python
import jax
import jax.numpy as jnp
import numpy as np
from jax import lax
from jax.experimental import pallas as pl
from jax.experimental.pallas import tpu as pltpu
from jax.sharding import PartitionSpec as P


EPS = 1e-05
BF = jnp.bfloat16
F32 = jnp.float32

ROWS = 32
CAP = 10
HALF = 2
TOK = ROWS * HALF
EXP = 32
USED = CAP * HALF
LANE = 128
LINES = 8
PACK = EXP * LINES
REST = USED - 2 * LINES
ALL = EXP * USED
PARTS = ((0, PACK), (PACK, ALL - PACK))


def dot(a, b):
    return lax.dot_general(a, b, (((1,), (0,)), ((), ())), preferred_element_type=F32)


def dot_t0(a, b):
    return lax.dot_general(a, b, (((0,), (0,)), ((), ())), preferred_element_type=F32)


def dot_t1(a, b):
    return lax.dot_general(a, b, (((1,), (1,)), ((), ())), preferred_element_type=F32)


def split2(v):
    hi = v.astype(BF)
    return hi, (v - hi.astype(F32)).astype(BF)


def split3(v):
    hi = v.astype(BF)
    rest = v - hi.astype(F32)
    mid = rest.astype(BF)
    return hi, mid, (rest - mid.astype(F32)).astype(BF)


def flags(test):
    return jnp.where(test, 1.0, 0.0).astype(BF)


def count(shape, axis):
    return lax.broadcasted_iota(jnp.int32, shape, axis).astype(F32)


def over(v, by):
    whole = jnp.floor((v + 0.5) * (1.0 / by))
    return whole, v - by * whole


def row_place(first, shape, axis):
    s = count(shape, axis) + first
    group, inner = over(s, PACK)
    source, line = over(inner, LINES)
    source_rest, line_rest = over(inner, REST)
    rest = group >= 2
    return jnp.where(rest, source_rest, source), jnp.where(rest, line_rest, line) + LINES * group


def line_place(shape, axis):
    return over(count(shape, axis), LINES)


def column_place(shape, axis):
    group, inner = over(count(shape, axis), PACK)
    partner, line = over(inner, LINES)
    slot = jnp.where(group >= 3, jnp.where(line >= REST, line + (2 * LINES - REST), -9.0), line + LINES * group)
    return partner, slot


def expand_of():
    shape = (EXP, 4 * PACK)
    return flags(column_place(shape, 1)[0] == count(shape, 0))


def expand_t_of():
    shape = (4 * PACK, EXP)
    return flags(column_place(shape, 0)[0] == count(shape, 1))


def mask_of(picks):
    shape = (EXP, ROWS)
    experts = lax.broadcasted_iota(jnp.int32, shape, 0)
    same = flags(experts == lax.broadcasted_iota(jnp.int32, shape, 1))
    masks = []
    for v in picks:
        mask = jnp.zeros(shape, F32)
        for k in range(v.shape[0]):
            mask = mask + jnp.where(v[k : k + 1, :] == experts, 1.0, 0.0)
        masks.append(dot_t0(mask.astype(BF), same))
    return jnp.concatenate(masks, axis=0)


def slots_of(mask, expand):
    row = lax.broadcasted_iota(jnp.int32, (TOK, TOK), 0)
    column = lax.broadcasted_iota(jnp.int32, (TOK, TOK), 1)
    earlier = flags((column < row) & ((row < ROWS) | (column >= ROWS)))
    start = jnp.where(lax.broadcasted_iota(jnp.int32, (TOK, EXP), 0) < ROWS, 0.0, 1.0 * CAP)
    slot = mask * (dot(earlier, mask.astype(BF)) + start + 1.0) - 1.0
    table = dot(slot.astype(BF), expand) == column_place((1, 4 * PACK), 1)[1]
    return table, slot


def norm(tokens, gain):
    values = tokens.astype(F32)
    scale = lax.rsqrt(jnp.mean(values * values, axis=-1, keepdims=True) + EPS)
    return (values * scale * gain).astype(BF), scale, values


def mix(normed, router, mask):
    logits = dot_t1(normed, router)
    expo = jnp.where(mask > 0.0, jnp.exp(jnp.where(mask > 0.0, logits, 0.0)), 0.0)
    return expo / jnp.sum(expo, axis=-1, keepdims=True)


def weighted(table, parts, expand):
    return [jnp.where(table, dot(v, expand), 0.0).astype(BF) for v in parts]


def to_packed(picked, rows, out, done, first=0):
    half = rows.shape[1] // 2
    width = 2 * half
    for i in range(2):
        columns = slice(i * PACK, (i + 1) * PACK)
        out[:, first + i * width : first + (i + 1) * width] = sum(dot_t0(v[:, columns], rows) for v in picked).astype(BF)
        done(i)
    low, high = slice(2 * PACK, 3 * PACK), slice(3 * PACK, 4 * PACK)
    last = sum(dot_t0(v[:, low], rows[:, :half]) + dot_t0(v[:, high], rows[:, half:]) for v in picked)
    out[:, first + 2 * width : first + 2 * width + half] = last.astype(BF)
    done(2)


def from_packed(picked, packed, width):
    half = width // 2
    rest = packed[:, 2 * width : 2 * width + half]
    total = sum(
        dot(v[:, :PACK], packed[:, :width]) + dot(v[:, PACK : 2 * PACK], packed[:, width : 2 * width]) for v in picked
    )
    low = sum(dot(v[:, 2 * PACK : 3 * PACK], rest) for v in picked)
    high = sum(dot(v[:, 3 * PACK :], rest) for v in picked)
    return total + jnp.concatenate([low, high], axis=1)


def rest_tables():
    shape = (EXP * REST, PACK)
    source, line = over(count(shape, 0), REST)
    place, at = line_place(shape, 1)
    return flags((source == place) & (line == at)), flags((source == place) & (line + REST == at))


def unpack(packed, first, width, out, piece):
    if piece == 0:
        out[0:PACK, :] = packed[:, first : first + width]
        return
    half = width // 2
    out[PACK : 2 * PACK, :] = packed[:, first + width : first + 2 * width]
    rest = packed[:, first + 2 * width : first + 2 * width + half]
    low, high = rest_tables()
    out[2 * PACK :, :half] = dot(low, rest).astype(BF)
    out[2 * PACK :, half:] = dot(high, rest).astype(BF)


def pack(rows, out, piece):
    width = rows.shape[1]
    if piece == 0:
        out[:, :width] = rows
        return
    half = width // 2
    out[:, width : 2 * width] = rows[:PACK, :]
    low, high = rest_tables()
    rest = dot_t0(low, rows[PACK:, :half]) + dot_t0(high, rows[PACK:, half:])
    out[:, 2 * width : 2 * width + half] = rest.astype(BF)


def line_table(first, number, test):
    shape = (number, PACK)
    source, line = line_place(shape, 1)
    return flags((row_place(first, shape, 0)[0] == source) & test(line))


def slot_lanes(first, number):
    shape = (number, LANE)
    return row_place(first, shape, 0)[1] == count(shape, 1)


def column_of(small, first, number, test):
    wide = dot(line_table(first, number, test), small)
    return jnp.sum(jnp.where(slot_lanes(first, number), wide, 0.0), axis=1, keepdims=True)


def small_lines(masked):
    shape = (3 * PACK, LANE)
    place = flags(column_place(shape, 0)[1] == count(shape, 1))
    shape = (PACK, 3 * PACK)
    source, line = line_place(shape, 0)
    same = source == column_place(shape, 1)[0]
    total = None
    for i, v in enumerate(masked):
        row = jnp.sum(v[:, : 3 * PACK].astype(F32), axis=0, keepdims=True)
        part = dot(jnp.where(same & (line == i), row, 0.0).astype(BF), place)
        total = part if total is None else total + part
    return total.astype(BF)


def cost(flops, arrays):
    size = sum(int(np.prod(a.shape)) * jnp.dtype(a.dtype).itemsize for a in arrays)
    return pl.CostEstimate(flops=flops, bytes_accessed=size, transcendentals=0)


def cuts(sizes):
    return [(sum(sizes[:i]), size) for i, size in enumerate(sizes)]


def view(ref, axis, cut):
    return ref.at[(slice(None),) * axis + (pl.ds(*cut),)]


class Load:
    def __init__(self, array, sizes=None, axis=0, first=0, width=None):
        self.array, self.axis, self.first = array, axis, first
        self.width = width or array.shape[-1]
        self.shape = tuple(array.shape[:-1]) + (self.width,)
        self.dtype = array.dtype
        self.cuts = cuts(sizes or (self.shape[axis],))
        self.other = None

    def copies(self, src, dst, sem, at):
        if self.width != self.array.shape[-1]:
            src = view(src, len(self.shape) - 1, (self.first, self.width))
        return [
            pltpu.make_async_copy(view(src, self.axis, cut), view(dst, self.axis, cut), sem.at[i])
            for i, cut in enumerate(self.cuts)
        ]


class Tokens(Load):
    def __init__(self, array):
        super().__init__(array)
        self.shape = (TOK, array.shape[1])
        self.cuts = [(0, TOK)]

    def copies(self, src, dst, sem, at):
        return [pltpu.make_async_copy(src.at[pl.ds(pl.multiple_of(at[0] * TOK, TOK), TOK)], dst, sem.at[0])]


class Either(Load):
    def __init__(self, array, other, sizes):
        super().__init__(array, sizes)
        self.other = other


class Moves:
    def __init__(self, loads, stores):
        self.loads, self.stores, self.taken = loads, stores, set()

    def start(self, order):
        for i, piece in order or [(i, p) for i, load in enumerate(self.loads) for p in range(len(load))]:
            self.loads[i][piece].start()

    def need(self, *names):
        for name in names:
            i, piece = name if isinstance(name, tuple) else (name, None)
            for p in range(len(self.loads[i])) if piece is None else [piece]:
                if (i, p) not in self.taken:
                    self.taken.add((i, p))
                    self.loads[i][p].wait()

    def flush(self, piece, *outs):
        for j in outs:
            self.stores[j][piece].start()

    def end(self):
        self.need(*range(len(self.loads)))
        for store in self.stores:
            for copy in store:
                copy.wait()


def call(body, outs, args, flops, scratch=(), order=None):
    args = [v if isinstance(v, Load) else Load(v) for v in args]
    others = [v.other for v in args if v.other is not None]
    out_shape = [jax.ShapeDtypeStruct(out[0], out[1]) for out in outs]
    ways = [(out[2], cuts(out[3])) if len(out) > 2 else (0, [(0, out[0][0])]) for out in outs]
    n, m = len(args), len(outs)

    def kernel(*refs):
        where = (lax.axis_index("pipe"), lax.axis_index("dp"))
        ins, twins, refs = refs[:n], refs[n : n + len(others)], refs[n + len(others) :]
        results, held, refs = refs[:m], refs[m : m + n], refs[m + n :]
        made, load_sems, store_sems = refs[:m], refs[m : m + n], refs[m + n : m + n + m]
        own = refs[m + n + m :]
        loads = [v.copies(src, dst, sem, where) for v, src, dst, sem in zip(args, ins, held, load_sems)]
        stores = [
            [
                pltpu.make_async_copy(view(made[j], axis, cut), view(results[j], axis, cut), store_sems[j].at[i])
                for i, cut in enumerate(pieces)
            ]
            for j, (axis, pieces) in enumerate(ways)
        ]
        moves = Moves(loads, stores)
        if others:
            second = iter(twins)
            second = [src if v.other is None else next(second) for v, src in zip(args, ins)]
            for pick, sources in enumerate((ins, second)):

                @pl.when(where[0] == pick)
                def _():
                    picked = [v.copies(*way, where) for v, *way in zip(args, sources, held, load_sems)]
                    for piece in range(max(len(copies) for copies in picked)):
                        for copies in picked:
                            if piece < len(copies):
                                copies[piece].start()

        else:
            moves.start(order)
        body(moves, where, held, made, *own)
        moves.end()

    hbm = pl.BlockSpec(memory_space=pl.ANY)
    return pl.pallas_call(
        kernel,
        out_shape=out_shape,
        in_specs=[hbm] * (n + len(others)),
        out_specs=[hbm] * m,
        scratch_shapes=[pltpu.VMEM(v.shape, v.dtype) for v in args]
        + [pltpu.VMEM(s.shape, s.dtype) for s in out_shape]
        + [pltpu.SemaphoreType.DMA((len(v.cuts),)) for v in args]
        + [pltpu.SemaphoreType.DMA((len(pieces),)) for axis, pieces in ways]
        + list(scratch),
        cost_estimate=cost(flops, [v.array for v in args] + out_shape),
        compiler_params=pltpu.CompilerParams(vmem_limit_bytes=63 << 20),
    )(*[v.array for v in args], *others)


def start_body(moves, at, ins, outs):
    inputs, cotangent, picks_own, picks_other, gain_own, gain_other, router_own, router_other = ins
    send, weights, tokens, grad, gains, routers, mask0_out, mask1_out = outs
    mine = at[0] == 0
    expand = expand_of()
    moves.need(2, 3)
    own = [picks_own[HALF * at[0] + i] for i in range(HALF)]
    other = [picks_other[HALF * at[0] + i] for i in range(HALF)]
    mask = mask_of([jnp.where(mine, v, w) for v, w in zip(own, other)])
    mask1 = mask_of([jnp.where(mine, w, v) for v, w in zip(own, other)])
    mask0_out[...] = mask
    mask1_out[...] = mask1
    table0 = slots_of(mask, expand)[0]
    table1 = slots_of(mask1, expand)[0]
    moves.need(0, 1, 4, 5)
    own, other = gain_own[...], gain_other[...]
    gain0 = jnp.where(mine, own, other)
    gains[0:1, :] = gain0
    gains[1:2, :] = jnp.where(mine, other, own)
    token, cot = inputs[...], cotangent[...]
    normed, _, _ = norm(token, gain0)
    to_packed([flags(table0)], normed, send, lambda i: moves.flush(i, 0))
    to_packed([flags(table1)], cot, send, lambda i: moves.flush(3 + i, 0), send.shape[1] // 2)
    tokens[...] = token
    grad[...] = cot
    moves.need(6, 7)
    own, other = router_own[...], router_other[...]
    router0 = jnp.where(mine, own, other)
    routers[0:EXP, :] = router0
    routers[EXP:, :] = jnp.where(mine, other, own)
    weights[...] = mix(normed, router0, mask)
    moves.flush(0, 1, 2, 3, 4, 5, 6, 7)


def forward_body(moves, at, ins, outs, rows):
    x, wg, wu, wd = ins
    (out,) = outs
    width = rows.shape[1]
    for i, (first, number) in enumerate(PARTS):
        part = pl.ds(first, number)
        moves.need(*[(0, 0)] if i == 0 else [(0, 1), (0, 2)])
        unpack(x, 0, width, rows, i)
        moves.need(1)
        gate = dot(rows[part, :], wg[...])
        moves.need(2)
        up = dot(rows[part, :], wu[...])
        hidden = (jax.nn.silu(gate) * up).astype(BF)
        moves.need(3)
        pack(dot(hidden, wd[...]).astype(BF), out, i)
        for piece in [0] if i == 0 else [1, 2]:
            moves.flush(piece, 0)


def residual_body(moves, at, ins, outs):
    x, wg, wu = ins
    fa, fb, hid, rows, grad = outs
    width = rows.shape[1]
    for i, (first, number) in enumerate(PARTS):
        part = pl.ds(first, number)
        moves.need(0, 1)
        unpack(x, 0, width, rows, i)
        unpack(x, x.shape[1] // 2, width, grad, i)
        gate = dot(rows[part, :], wg[...])
        moves.need(2)
        up = dot(rows[part, :], wu[...])
        sig = jax.nn.sigmoid(gate)
        act = gate * sig
        hid[part, :] = (act * up).astype(BF)
        fb[part, :] = act
        fa[part, :] = up * sig * (1.0 + gate * (1.0 - sig))
        moves.flush(i, 0, 1, 2, 3, 4)


def expert1_body(moves, at, ins, outs):
    x, g, wg, wu, wd = ins
    send, rows, scaled_out, gate_out, up_out, hid = outs
    width = rows.shape[1]
    moves.need(0)
    small = x[:, x.shape[1] - LANE :]
    told = [jnp.zeros((PACK, LANE), F32) for _ in range(3)]
    for i, (first, number) in enumerate(PARTS):
        part = pl.ds(first, number)
        unpack(x, 0, width, rows, i)
        moves.need(2)
        gate = dot(rows[part, :], wg[...])
        moves.need(3)
        up = dot(rows[part, :], wu[...])
        sig = jax.nn.sigmoid(gate)
        act = gate * sig
        hidden = (act * up).astype(BF)
        hid[part, :] = hidden
        moves.need(4)
        out = dot(hidden, wd[...]).astype(BF)
        weight = column_of(small, first, number, lambda line: line < 2)
        moves.need((1, i))
        grad = g[part, :].astype(F32)
        weight_grad = jnp.sum(grad * out.astype(F32), axis=1, keepdims=True)
        scaled = (weight * grad).astype(BF)
        scaled_out[part, :] = scaled
        grad_hidden = dot_t1(scaled, wd[...])
        gate_back = (grad_hidden * (up * sig * (1.0 + gate * (1.0 - sig)))).astype(BF)
        up_back = (grad_hidden * act).astype(BF)
        gate_out[part, :] = gate_back
        up_out[part, :] = up_back
        pack((dot_t1(gate_back, wg[...]) + dot_t1(up_back, wu[...])).astype(BF), send, i)
        placed = jnp.where(slot_lanes(first, number), weight_grad, 0.0)
        for k, v in enumerate(split3(placed)):
            told[k] = told[k] + dot_t0(line_table(first, number, lambda line: line == k), v)
        moves.flush(i, 1, 2, 3, 4, 5)
        if i == 0:
            moves.flush(0, 0)
    send[:, send.shape[1] - LANE :] = (told[0] + told[1] + told[2]).astype(BF)
    moves.flush(1, 0)
    moves.flush(2, 0)


def blocks_of(gb, ub, x, sc, hid, group, which, out):
    half, quarter = x.shape[1] // 2, x.shape[1] // 4
    rows = x[:, pl.ds(pl.multiple_of(group * half + which * quarter, quarter), quarter)]
    gate = dot_t0(rows, gb[...])
    up = dot_t0(rows, ub[...])
    out[0:quarter, :] = gate.astype(BF)
    out[quarter : 2 * quarter, :] = up.astype(BF)
    low = hid[:, pl.ds(pl.multiple_of(which * quarter, quarter), quarter)]
    wide = sc[:, pl.ds(pl.multiple_of(group * half, half), half)]
    out[2 * quarter :, :] = dot_t0(low, wide).astype(BF)
    return gate, up


def four_blocks(at):
    return [(group, which) for group in (1 - at[1], at[1]) for which in (1 - at[0], at[0])]


def grads1_body(moves, at, ins, outs):
    gb, ub, x, sc, hid = ins
    moves.need(0, 1, 2, 3, 4)
    for j, (group, which) in enumerate(four_blocks(at)):
        blocks_of(gb, ub, x, sc, hid, group, which, outs[j])
        moves.flush(0, j)


def backward0_body(moves, at, ins, outs, rows, gb, ub, total):
    sc, fa, fb, wd, x, hid, wg, wu, x1, layer_gains, gains = ins
    mine, theirs = outs[4:]
    width = rows.shape[1]
    moves.need(3)
    for i, (first, number) in enumerate(PARTS):
        part = pl.ds(first, number)
        moves.need(*[(0, 0)] if i == 0 else [(0, 1), (0, 2)])
        moves.need((1, i), (2, i))
        unpack(sc, 0, width, rows, i)
        grad_hidden = dot_t1(rows[part, :], wd[...])
        gb[part, :] = (grad_hidden * fa[part, :]).astype(BF)
        ub[part, :] = (grad_hidden * fb[part, :]).astype(BF)
    moves.need(4, 5, 6, 7)
    half, quarter = width // 2, width // 4
    shape = (quarter, quarter)
    same = lax.broadcasted_iota(jnp.int32, shape, 0) == lax.broadcasted_iota(jnp.int32, shape, 1)
    for j, (group, which) in enumerate(four_blocks(at)):
        gate, up = blocks_of(gb, ub, x, rows, hid, group, which, outs[j])
        moves.flush(0, j)
        place = pl.ds(pl.multiple_of(group * half + which * quarter, quarter), quarter)
        column = jnp.sum(gate * wg[place, :].astype(F32) + up * wu[place, :].astype(F32), axis=1, keepdims=True)
        total[1:2, place] = jnp.sum(jnp.where(same, column, 0.0), axis=0, keepdims=True)
    moves.need(8, 9, 10)
    small = sc[:, sc.shape[1] - LANE :]
    for line, array, index in ((0, x, 0), (2, x1, 1)):
        column = column_of(small, 0, ALL, lambda at_line: at_line == index)
        wide = jnp.broadcast_to(column, (ALL, LANE)).astype(BF)
        total[line : line + 1, :] = dot_t0(wide, array[...])[0:1, :]
    gain0 = total[1:2, :] / layer_gains[0:1, :] + gains[1:2, :]
    gain1 = gains[0:1, :]
    first = at[0] == 0
    column0, column1 = total[0:1, :], total[2:3, :]
    mine[0:1, :] = jnp.where(first, column0, column1)
    mine[1:2, :] = jnp.where(first, gain0, gain1)
    theirs[0:1, :] = jnp.where(first, column1, column0)
    theirs[1:2, :] = jnp.where(first, gain1, gain0)
    moves.flush(0, 4, 5)


def told_body(moves, at, ins, outs):
    own, other = ins
    (out,) = outs
    moves.need(0, 1)
    group, lines, lane = out.shape
    both = own[...] + other[...]
    for v in range(2):
        for j in range(lines // 2):
            piece = both[v : v + 1, j * lane : (j + 1) * lane]
            out[:, v * (lines // 2) + j, :] = jnp.broadcast_to(piece, (group, lane))
    moves.flush(0, 0)


def finish_body(moves, at, ins, outs):
    low, high, low_got, high_got, heard = ins
    router, gain = outs[3:]
    moves.need(4)
    _, lines, lane = heard.shape
    for j in range(lines // 2):
        column = slice(j * lane, (j + 1) * lane)
        router[:, column] = heard[0:EXP, j, :] + heard[EXP:, j, :]
        gain[:, column] = jnp.sum(heard[:, lines // 2 + j, :], axis=0, keepdims=True)
    moves.flush(0, 3, 4)
    quarter = low.shape[0] // 3
    for i, out in enumerate(outs[:3]):
        moves.need(*[(k, i) for k in range(4)])
        rows = slice(i * quarter, (i + 1) * quarter)
        out[0:quarter, :] = (low[rows, :].astype(F32) + low_got[rows, :].astype(F32)).astype(BF)
        out[quarter:, :] = (high[rows, :].astype(F32) + high_got[rows, :].astype(F32)).astype(BF)
        moves.flush(0, i)


def middle_body(moves, at, ins, outs):
    tokens, mask0, weights0, returned, mask1, gains, routers = ins
    mixed_out, send, weights1 = outs
    width = tokens.shape[1]
    expand = expand_of()
    moves.need(1, 2, 4)
    table0 = slots_of(mask0[...], expand)[0]
    parts = weighted(table0, split2(weights0[...]), expand)
    table1 = slots_of(mask1[...], expand)[0]
    moves.need(0, 3, 5, 6)
    mixed = (tokens[...].astype(F32) + from_packed(parts, returned, width)).astype(BF)
    mixed_out[...] = mixed
    normed, _, _ = norm(mixed, gains[1:2, :])
    weights = mix(normed, routers[EXP:, :], mask1[...])
    weights1[...] = weights
    send[:, send.shape[1] - LANE :] = small_lines(weighted(table1, split2(weights), expand))
    to_packed([flags(table1)], normed, send, lambda i: moves.flush(i, 1))
    moves.flush(0, 0, 2)


def turn_body(moves, at, ins, outs):
    tokens1, mask1, weights1, returned1, grad, tokens0, mask0, weights0, returned0, gains, routers = ins
    send, gains_out = outs
    width = tokens1.shape[1]
    half = width // 2
    expand = expand_of()
    moves.need(0, 1, 2, 4, 5, 6, 7, 9, 10)
    gain0, gain1 = gains[0:1, :], gains[1:2, :]
    table1, slot1 = slots_of(mask1[...], expand)
    table0 = slots_of(mask0[...], expand)[0]
    w0, w1 = weights0[...], weights1[...]
    parts0 = weighted(table0, split2(w0), expand)
    _, scale0, values0 = norm(tokens0[...], gain0)
    _, scale1, values1 = norm(tokens1[...], gain1)
    moves.need(3)
    expert_part = from_packed([flags(table1)], returned1, width)
    shape = (PACK, EXP)
    source, line = line_place(shape, 0)
    told = dot_t0(returned1[:, returned1.shape[1] - LANE :], flags((source == count(shape, 1)) & (line < 3)))
    wg1 = jnp.zeros((TOK, EXP), F32)
    for i in range(USED):
        wg1 = jnp.where(slot1 == i, told[i : i + 1, :], wg1)
    lg1 = (w1 * (wg1 - jnp.sum(w1 * wg1, axis=-1, keepdims=True))).astype(BF)
    normed_grad1 = dot(lg1, routers[EXP:, :]) + expert_part
    gains_out[0:1, :] = jnp.sum(normed_grad1 * values1 * scale1, axis=0, keepdims=True)
    q = normed_grad1 * gain1
    grad_f = grad[...].astype(F32)
    g0 = (
        grad_f + scale1 * q - scale1 * scale1 * scale1 * values1 * jnp.mean(q * values1, axis=-1, keepdims=True)
    ).astype(BF)
    moves.need(8)
    rest = returned0[:, 2 * width : 2 * width + half]
    met = jnp.concatenate(
        [
            dot_t1(g0, returned0[:, :width]),
            dot_t1(g0, returned0[:, width : 2 * width]),
            dot_t1(g0[:, :half], rest),
            dot_t1(g0[:, half:], rest),
        ],
        axis=1,
    )
    met = jnp.where(table0, met, 0.0)
    expand_t = expand_t_of()
    wg0 = jnp.zeros((TOK, EXP), F32)
    for part in split3(met):
        wg0 = wg0 + dot(part, expand_t)
    lg0 = (w0 * (wg0 - jnp.sum(w0 * wg0, axis=-1, keepdims=True))).astype(BF)
    gains_out[1:2, :] = jnp.sum(dot(lg0, routers[0:EXP, :]) * values0 * scale0, axis=0, keepdims=True)
    lines = [weighted(table0, [lg0], expand)[0], weighted(table1, [lg1], expand)[0]]
    send[:, send.shape[1] - LANE :] = small_lines(lines)
    to_packed(parts0, g0, send, lambda i: moves.flush(i, 0))
    moves.flush(0, 1)


def exchanged(rows):
    return lax.all_to_all(rows, "expert", split_axis=0, concat_axis=0, tiled=True)


def swapped(value):
    return lax.ppermute(value, "pipe", [(0, 1), (1, 0)])


def shards(inputs, cotangent, norm_gain, w_router, w_gate, w_up, w_down, routes):
    pipe = lax.axis_index("pipe")
    width = inputs.shape[-1]
    inner = w_gate.shape[-1]
    half, quarter = width // 2, width // 4
    first = pipe == 0
    flops = ALL * width * inner

    def both(own, other):
        return jnp.where(first, own, other), jnp.where(first, other, own)

    picks = routes[0].transpose(0, 2, 1)
    router = w_router[0].T
    packed = 2 * width + half
    pieces = (width, width, half)
    with_small = (width, width, half + LANE)
    part_rows = [number for first, number in PARTS]
    rows_shape = ((ALL, width), BF, 0, part_rows)
    inner_shape = ((ALL, inner), BF, 0, part_rows)
    wide_shape = ((ALL, inner), F32, 0, part_rows)
    small_shape = ((PACK, packed + LANE), BF, 1, with_small)
    few = ((TOK, width), BF)
    send0, weights0, tokens0, grad1, gains, routers, mask0, mask1 = call(
        start_body,
        [((PACK, 2 * packed), BF, 1, pieces * 2), ((TOK, EXP), F32), few, few, ((2, width), F32), ((2 * EXP, width), BF)] + [((TOK, EXP), F32)] * 2,
        [
            Tokens(inputs.reshape(-1, width)),
            Tokens(cotangent.reshape(-1, width)),
            picks,
            swapped(picks),
            norm_gain,
            swapped(norm_gain),
            router,
            swapped(router),
        ],
        400_000_000,
    )
    arrived = exchanged(send0)
    mats = [both(w[0, 0], swapped(w[0, 0])) for w in (w_gate, w_up, w_down)]
    (gate0, gate1), (up0, up1), (down0, down1) = lax.optimization_barrier(mats)

    (out0,) = call(
        forward_body,
        [((PACK, packed), BF, 1, pieces)],
        [Load(arrived, pieces, 1, 0, packed), gate0, up0, down0],
        6 * flops,
        scratch=[pltpu.VMEM((ALL, width), BF)],
        order=[(0, 0), (1, 0), (2, 0), (3, 0), (0, 1), (0, 2)],
    )
    returned0 = exchanged(out0)
    fa0, fb0, hidden0, recv0, grad_rows = call(
        residual_body, [wide_shape, wide_shape, inner_shape, rows_shape, rows_shape], [arrived, gate0, up0], 4 * flops
    )

    tokens1, send1, weights1 = call(
        middle_body,
        [few, small_shape, ((TOK, EXP), F32)],
        [tokens0, mask0, weights0, returned0, mask1, gains, routers],
        600_000_000,
    )
    arrived1 = exchanged(send1)
    send_b, rows1, scaled1, gate_back1, up_back1, hidden1 = call(
        expert1_body,
        [small_shape, rows_shape, rows_shape, inner_shape, inner_shape, inner_shape],
        [arrived1, Load(grad_rows, part_rows), gate1, up1, down1],
        12 * flops,
        order=[(0, 0), (2, 0), (3, 0), (4, 0), (1, 0), (1, 1)],
    )
    returned1 = exchanged(send_b)

    block = ((3 * quarter, half), BF)

    def to_owner(paired, owner):
        return [
            lax.ppermute(paired, ("dp", "pipe"), [(2 * d + p, 2 * (1 - d) + owner) for d in range(2)]) for p in range(2)
        ]

    def paired_of(kept, swap):
        return (kept.astype(F32) + swap.astype(F32)).astype(BF)

    args1 = [gate_back1, up_back1, rows1, scaled1, hidden1]
    sent, kept, sent_near, kept_near = call(grads1_body, [block] * 4, args1, 6 * flops)
    paired1 = paired_of(kept, swapped(sent))
    got1 = to_owner(paired1, 1)

    send2, token_gains = call(
        turn_body,
        [small_shape, ((2, width), F32)],
        [tokens1, mask1, weights1, returned1, grad1, tokens0, mask0, weights0, returned0, gains, routers],
        900_000_000,
    )
    recv2 = exchanged(send2)
    sum1 = paired_of(kept_near, swapped(sent_near))
    low1 = lax.ppermute(sum1, "pipe", [(0, 1)])
    recv2, low1, sum1, got1 = lax.optimization_barrier((recv2, low1, sum1, got1))

    few_rows = ((2, width), F32)
    sent, kept, sent_near, kept_near, small, others = call(
        backward0_body,
        [block] * 4 + [few_rows] * 2,
        [Load(recv2, with_small, 1), Load(fa0, part_rows), Load(fb0, part_rows), down0, recv0, hidden0]
        + [gate0, up0, rows1, gains, token_gains],
        9 * flops,
        [pltpu.VMEM((ALL, width), BF), pltpu.VMEM((ALL, inner), BF), pltpu.VMEM((ALL, inner), BF)]
        + [pltpu.VMEM((8, width), F32)],
        order=[(3, 0), (0, 0), (1, 0), (2, 0), (0, 1), (0, 2), (1, 1), (2, 1)] + [(i, 0) for i in range(4, 11)],
    )
    paired0 = paired_of(kept, swapped(sent))
    got0 = to_owner(paired0, 0)
    told = call(told_body, [((2 * EXP, 2 * width // LANE, LANE), F32)], [small, swapped(others)], 1000)[0]
    heard = lax.all_to_all(told, ("dp", "expert"), split_axis=0, concat_axis=0, tiled=True)
    sum0 = paired_of(kept_near, swapped(sent_near))
    high0 = lax.ppermute(sum0, "pipe", [(1, 0)])
    thirds = (quarter,) * 3
    final = ((2 * quarter, half), BF)
    *outs, router_sum, gain_sum = call(
        finish_body,
        [final] * 3 + [((EXP, width), F32), ((1, width), F32)],
        [
            Either(sum0, low1, thirds),
            Either(high0, sum1, thirds),
            Either(got0[0], got1[0], thirds),
            Either(got0[1], got1[1], thirds),
            heard,
        ],
        1000,
    )
    return (
        outs[0][None, None],
        outs[1][None, None],
        outs[2][None, None],
        router_sum.T[None],
        gain_sum,
    )


def solution(mesh):
    in_specs = (
        P(None, ("dp", "expert"), None),
        P(None, ("dp", "expert"), None),
        P("pipe", None),
        P("pipe", None, None),
        P("pipe", "expert", None, None),
        P("pipe", "expert", None, None),
        P("pipe", "expert", None, None),
        P("pipe", None, ("dp", "expert"), None),
    )
    out_specs = (
        P("pipe", "expert", "dp", None),
        P("pipe", "expert", "dp", None),
        P("pipe", "expert", None, "dp"),
        P("pipe", None, None),
        P("pipe", None),
    )

    return jax.shard_map(shards, mesh=mesh, in_specs=in_specs, out_specs=out_specs, check_vma=False)
```
